512 devices in a mesh: gx: 8 (over y, core), gy: 16 (over z), ba: 4 (over x).
Axes of the slice: x: 4, y: 4, z: 16, core: 2. Of those that a mesh axis runs over, the one named last changes fastest.
Arguments:
- moved_fields: float32 [8, 16, 4, 16, 4, 4096], P('gx', 'gy', 'ba'), may hold values from -0.1 to 1.4, as said below
- send_slot: int32 [8, 16, 4, 16, 1], P('gx', 'gy', 'ba'), may hold values from -1 to 15, as said below
- recv_index: int32 [8, 16, 4, 2], P('gx', 'gy', 'ba'), may hold values from 0 to 15, as said below
- site_kind: int32 [128, 256, 128], P('gx', 'gy', 'ba'), may hold values from 0 to 3
Outputs:
- distributions: float32 [19, 128, 256, 128], P(None, 'gx', 'gy', 'ba')
The draws below stay inside these ranges and needn't reach their ends.
Inputs may be any that keep to these rules, and one draw needn't show every extreme that they name: Blocks move only between devices with the same gx and ba. Within such a group, the live entries of one device's send_slot are distinct slots; the entry [p, c] is live exactly when some device p' = p of the group has recv_index p_sender + c naming this device, and every device receives exactly 2 blocks, each from one live entry. A device sends at most 1 block to one peer; the number of live slots of a device varies. `recv_index`: entries are distinct within a device and consistent with send_slot as stated there. `moved_fields`: component 0 is the density, between 0.6 and 1.4; components 1 to 3 are velocities between -0.1 and 0.1; slots that no live send_slot entry names hold values of the same kind.
All inputs are finite; a program needn't handle non-finite values.
Results may differ from the reference program's by a relative error of at most 0.0003.
Values sent between devices are 32-bit elements; how exact they have to be, the bound alone decides.
No kernel may reach another device: no remote copies, remote signals or barrier semaphores. Data moves between devices by JAX's collectives and lax.ppermute only.
A program may use at most 64 MiB of HBM per device.

```python
import jax
import jax.numpy as jnp

BLOCK = 16
B_DEV = 2
STEPS = 4
CAP = 1
SLOTS = 16
NX = 128
NY = 256
NZ = 128
N_GX = 8
N_GY = 16
N_BA = 4


def route_group(group_key):
    bias_key, pick_key, slot_key = jax.random.split(group_key, 3)
    sources = jnp.arange(N_GY, dtype=jnp.int32)
    source_bias = jax.random.randint(bias_key, (N_GY,), 0, 4)
    pick_noise = jax.random.randint(pick_key, (N_GY, N_GY), 0, 1024)
    scores = (pick_noise + 1024 * source_bias[None, :]) * N_GY + sources[None, :]
    ranked_sources = jnp.argsort(-scores, axis=1).astype(jnp.int32)
    position = jnp.argsort(ranked_sources, axis=1).astype(jnp.int32)
    block_ids = jnp.arange(B_DEV, dtype=jnp.int32)
    receives = ranked_sources[:, block_ids % N_GY] * CAP + block_ids // N_GY
    rank_ids = jnp.arange(CAP, dtype=jnp.int32)
    is_live = position.T[:, :, None] + N_GY * rank_ids[None, None, :] < B_DEV
    live_flat = is_live.reshape(N_GY, N_GY * CAP)
    slot_noise = jax.random.randint(slot_key, (N_GY, N_GY * CAP), 0, 1048576) * (N_GY * CAP) + jnp.arange(N_GY * CAP, dtype=jnp.int32)[None, :]
    higher = (slot_noise[:, None, :] > slot_noise[:, :, None]) & live_flat[:, None, :]
    rank_live = jnp.sum(higher.astype(jnp.int32), axis=2)
    send_table = jnp.where(live_flat, SLOTS - 1 - rank_live, -1).reshape(N_GY, N_GY, CAP)
    return (send_table.astype(jnp.int32), receives.astype(jnp.int32))


def routes(base_key):
    group_keys = jax.random.split(jax.random.fold_in(base_key, 11), N_GX * N_BA)
    send_table, receives = jax.vmap(route_group)(group_keys)
    send_table = send_table.reshape(N_GX, N_BA, N_GY, N_GY, CAP).transpose(0, 2, 1, 3, 4)
    receives = receives.reshape(N_GX, N_BA, N_GY, B_DEV).transpose(0, 2, 1, 3)
    return (send_table, receives)


def draw_send_slot(key, part):
    return routes(key)[0]


def draw_recv_index(key, part):
    return routes(key)[1]


def draw_moved_fields(key, part):
    shape = (N_GX, N_GY, N_BA, SLOTS, BLOCK ** 3)
    density_key, speed_key = jax.random.split(jax.random.fold_in(key, 3))
    density = jax.random.uniform(density_key, shape, dtype=jnp.float32, minval=0.6, maxval=1.4)
    speeds = jax.random.uniform(speed_key, (3,) + shape, dtype=jnp.float32, minval=-0.1, maxval=0.1)
    stacked = jnp.concatenate([density[None], speeds], axis=0)
    return stacked.transpose(1, 2, 3, 4, 0, 5)


def draw_site_kind(key, part):
    base_key = jax.random.fold_in(key, 5)
    radius_key, center_key, present_key = jax.random.split(base_key, 3)
    columns_x = NX // BLOCK
    columns_y = NY // BLOCK
    top_radius = max(BLOCK // 2, 2)
    radius = jax.random.randint(radius_key, (columns_x, columns_y), 1, top_radius + 1)
    center_pick = jax.random.randint(center_key, (2, columns_x, columns_y), 0, 1048576)
    span = jnp.maximum(BLOCK - 2 * radius + 1, 1)
    center_x = radius + center_pick[0] % span
    center_y = radius + center_pick[1] % span
    present = jax.random.randint(present_key, (columns_x, columns_y), 0, 4) > 0
    site_x = jnp.arange(NX, dtype=jnp.int32)
    site_y = jnp.arange(NY, dtype=jnp.int32)
    column_x = site_x // BLOCK
    column_y = site_y // BLOCK
    local_x = site_x % BLOCK
    local_y = site_y % BLOCK
    radius_here = radius[column_x][:, column_y]
    cx_here = center_x[column_x][:, column_y]
    cy_here = center_y[column_x][:, column_y]
    present_here = present[column_x][:, column_y]
    offset_x = local_x[:, None] - cx_here
    offset_y = local_y[None, :] - cy_here
    distance = offset_x * offset_x + offset_y * offset_y
    inside = (distance < radius_here * radius_here) & present_here
    site_z = jnp.arange(NZ, dtype=jnp.int32)[None, None, :]
    inside3 = inside[:, :, None]
    kinds = jnp.where(inside3, jnp.where(site_z == 0, 2, jnp.where(site_z == NZ - 1, 3, 0)), 1)
    return kinds.astype(jnp.int32)


def setup_inputs(seed: int = 0) -> dict:
    seeds = jax.random.split(jax.random.key(seed), 5)
    moved_fields = draw_moved_fields(jax.random.fold_in(seeds[4], 71), 0)
    send_slot = draw_send_slot(jax.random.fold_in(seeds[4], 71), 0)
    recv_index = draw_recv_index(jax.random.fold_in(seeds[4], 71), 0)
    site_kind = draw_site_kind(jax.random.fold_in(seeds[4], 71), 0)
    return {"moved_fields": moved_fields, "send_slot": send_slot, "recv_index": recv_index, "site_kind": site_kind}


VELOCITIES = ((0, 0, 0), (1, 0, 0), (-1, 0, 0), (0, 1, 0), (0, -1, 0), (0, 0, 1), (0, 0, -1),
              (1, 1, 0), (-1, -1, 0), (1, -1, 0), (-1, 1, 0), (1, 0, 1), (-1, 0, -1),
              (1, 0, -1), (-1, 0, 1), (0, 1, 1), (0, -1, -1), (0, 1, -1), (0, -1, 1))
WEIGHTS = (1.0 / 3.0,) + (1.0 / 18.0,) * 6 + (1.0 / 36.0,) * 12
OPPOSITE = (0, 2, 1, 4, 3, 6, 5, 8, 7, 10, 9, 12, 11, 14, 13, 16, 15, 18, 17)
RELAX_RATE = 1.25
INLET_SPEED = 0.05


def dotted(vector, speeds):
    running = None
    for sign_value, component in zip(vector, speeds):
        if sign_value != 0:
            signed_term = component if sign_value > 0 else -component
            running = signed_term if running is None else running + signed_term
    return running


def equilibrium_one(direction_id, density, speeds, squared):
    baseline = 1.0 - 1.5 * squared
    projected = dotted(VELOCITIES[direction_id], speeds)
    if projected is None:
        return WEIGHTS[direction_id] * density * baseline
    return WEIGHTS[direction_id] * density * (baseline + 3.0 * projected + 4.5 * projected * projected)


def square_of(speeds):
    return speeds[0] * speeds[0] + speeds[1] * speeds[1] + speeds[2] * speeds[2]


def collide(populations, site_kind):
    density = populations[0]
    for member in populations[1:]:
        density = density + member
    speeds = []
    for axis_id in range(3):
        momentum = None
        for vector, member in zip(VELOCITIES, populations):
            if vector[axis_id] != 0:
                signed_term = member if vector[axis_id] > 0 else -member
                momentum = signed_term if momentum is None else momentum + signed_term
        speeds.append(momentum / density)
    squared = square_of(speeds)
    inlet_speeds = (0.0, 0.0, INLET_SPEED)
    inlet_squared = square_of(inlet_speeds)
    result = []
    for direction_id in range(19):
        balanced = equilibrium_one(direction_id, density, speeds, squared)
        outflow = equilibrium_one(direction_id, 1.0, speeds, squared)
        inflow = equilibrium_one(direction_id, 1.0, inlet_speeds, inlet_squared)
        relaxed = populations[direction_id] + RELAX_RATE * (balanced - populations[direction_id])
        updated = jnp.where(site_kind == 3, outflow, relaxed)
        updated = jnp.where(site_kind == 2, inflow, updated)
        updated = jnp.where(site_kind == 1, populations[OPPOSITE[direction_id]], updated)
        result.append(updated)
    return result


def initial_populations(fields):
    speeds = (fields[1], fields[2], fields[3])
    squared = square_of(speeds)
    return [equilibrium_one(direction_id, fields[0], speeds, squared) for direction_id in range(19)]


def rebalance(moved_fields, send_slot, recv_index):
    gx_ids = jnp.arange(N_GX, dtype=jnp.int32)[:, None, None, None]
    gy_ids = jnp.arange(N_GY, dtype=jnp.int32)[None, :, None, None]
    ba_ids = jnp.arange(N_BA, dtype=jnp.int32)[None, None, :, None]
    senders = (recv_index // CAP).astype(jnp.int32)
    sender_rank = (recv_index % CAP).astype(jnp.int32)
    slot_ids = send_slot[gx_ids, senders, ba_ids, gy_ids, sender_rank]
    blocks = moved_fields[gx_ids, senders, ba_ids, slot_ids]
    blocks = blocks.reshape(N_GX, N_GY, N_BA, B_DEV, 4, BLOCK, BLOCK, BLOCK)
    blocks = blocks.transpose(4, 0, 5, 1, 6, 2, 3, 7)
    return blocks.reshape(4, N_GX * BLOCK, N_GY * BLOCK, N_BA * B_DEV * BLOCK)


def reference(moved_fields, send_slot, recv_index, site_kind):
    fields = rebalance(moved_fields, send_slot, recv_index)
    populations = initial_populations(fields)
    for step_id in range(STEPS):
        collided = collide(populations, site_kind)
        populations = [jnp.roll(member, vector, axis=(0, 1, 2)) for member, vector in zip(collided, VELOCITIES)]
    return jnp.stack(populations)
```

```python
import jax
import jax.numpy as jnp
from jax import lax
from jax.experimental import pallas as pl
from jax.experimental.pallas import tpu as pltpu
from jax.sharding import PartitionSpec as P

STEPS = 4
HALO = 4

VELOCITIES = (
    (0, 0, 0),
    (1, 0, 0),
    (-1, 0, 0),
    (0, 1, 0),
    (0, -1, 0),
    (0, 0, 1),
    (0, 0, -1),
    (1, 1, 0),
    (-1, -1, 0),
    (1, -1, 0),
    (-1, 1, 0),
    (1, 0, 1),
    (-1, 0, -1),
    (1, 0, -1),
    (-1, 0, 1),
    (0, 1, 1),
    (0, -1, -1),
    (0, 1, -1),
    (0, -1, 1),
)
WEIGHTS = (1.0 / 3.0,) + (1.0 / 18.0,) * 6 + (1.0 / 36.0,) * 12
OPPOSITE = (0, 2, 1, 4, 3, 6, 5, 8, 7, 10, 9, 12, 11, 14, 13, 16, 15, 18, 17)
RELAX_RATE = 1.25
INLET_SPEED = 0.05

SEG = 40
F32 = jnp.float32


def shifted_pairs(axis, step):
    devices = lax.axis_size(axis)
    return [(i, (i + step) % devices) for i in range(devices)]


def from_before(array, axis):
    return lax.ppermute(array, axis, shifted_pairs(axis, 1))


def from_after(array, axis):
    return lax.ppermute(array, axis, shifted_pairs(axis, -1))


def lane_ids():
    return lax.broadcasted_iota(jnp.int32, (8, 128), 1)


def row_ids():
    return lax.broadcasted_iota(jnp.int32, (8, 128), 0)


def roll_lanes(value, amount):
    amount = amount % 128
    return value if amount == 0 else pltpu.roll(value, amount, 1)


def roll_rows(value, amount):
    amount = amount % 8
    return value if amount == 0 else pltpu.roll(value, amount, 0)


def gather_kernel(wanted, held, out, sems):
    copies = []
    for peer in range(out.shape[0]):
        slot = jnp.maximum(wanted[peer], 0)
        copies.append(pltpu.make_async_copy(held.at[slot], out.at[peer], sems.at[peer]))
    for copy in copies:
        copy.start()
    for copy in copies:
        copy.wait()


def gather_blocks(wanted, held):
    peers = wanted.shape[0]
    return pl.pallas_call(
        gather_kernel,
        out_shape=jax.ShapeDtypeStruct((peers, 128, 128), F32),
        in_specs=[
            pl.BlockSpec(memory_space=pltpu.SMEM),
            pl.BlockSpec(memory_space=pl.ANY),
        ],
        out_specs=pl.BlockSpec(memory_space=pltpu.VMEM),
        scratch_shapes=[pltpu.SemaphoreType.DMA((peers,))],
        name="gather_blocks",
    )(wanted, held)


def pick_kernel(senders, arrived, blocks, low, high, sems):
    copies = []
    for block in range(2):
        copies.append(
            pltpu.make_async_copy(arrived.at[senders[block]], blocks.at[block], sems.at[block])
        )
    for copy in copies:
        copy.start()
    for copy in copies:
        copy.wait()
    part = (lane_ids() % 16) // 4
    for group in range(4):
        first = None
        last = None
        for quarter in range(4):
            rows = pl.ds((group * 4 + quarter) * 8, 8)
            near = roll_lanes(blocks[0, rows, :], 4 * quarter)
            far = roll_lanes(blocks[1, rows, :], 4 * quarter - 12)
            first = near if first is None else jnp.where(part == quarter, near, first)
            last = far if last is None else jnp.where(part == quarter, far, last)
        low[group] = first
        high[group] = last


def pick_blocks(senders, arrived):
    return pl.pallas_call(
        pick_kernel,
        out_shape=(
            jax.ShapeDtypeStruct((2, 128, 128), F32),
            jax.ShapeDtypeStruct((4, 8, 128), F32),
            jax.ShapeDtypeStruct((4, 8, 128), F32),
        ),
        in_specs=[
            pl.BlockSpec(memory_space=pltpu.SMEM),
            pl.BlockSpec(memory_space=pl.ANY),
        ],
        out_specs=(pl.BlockSpec(memory_space=pltpu.VMEM),) * 3,
        scratch_shapes=[pltpu.SemaphoreType.DMA((2,))],
        name="pick_blocks",
    )(senders, arrived)


def row_tiles(blocks, below, above, x_low, x_high):
    entries = []
    for column in range(24):
        if column < 4:
            entries.append((x_low[column], x_low[4 + column]))
        elif column < 20:
            rows = pl.ds((column - 4) * 8, 8)
            entries.append((blocks[0, rows, :], blocks[1, rows, :]))
        else:
            entries.append((x_high[column - 20], x_high[column - 16]))
    for group in range(6):
        if group == 0:
            entries.append((x_low[8], x_low[9]))
        elif group < 5:
            entries.append((below[group - 1], above[group - 1]))
        else:
            entries.append((x_high[8], x_high[9]))
    return entries


def side_kernel(blocks, below, above, x_low, x_high, down, up):
    left = lane_ids() < 64
    top = row_ids() < 4
    entries = row_tiles(blocks, below, above, x_low, x_high)
    for pair in range(15):
        first, second = entries[2 * pair], entries[2 * pair + 1]
        a = jnp.where(left, first[0], roll_lanes(first[1], 64))
        b = jnp.where(left, second[0], roll_lanes(second[1], 64))
        down[pl.ds(8 * pair, 8), :] = jnp.where(top, a, roll_rows(b, 4))
        a = jnp.where(left, roll_lanes(first[0], 64), first[1])
        b = jnp.where(left, roll_lanes(second[0], 64), second[1])
        up[pl.ds(8 * pair, 8), :] = jnp.where(top, roll_rows(a, 4), b)


def side_messages(blocks, below, above, x_low, x_high):
    return pl.pallas_call(
        side_kernel,
        out_shape=(jax.ShapeDtypeStruct((120, 128), F32),) * 2,
        in_specs=[pl.BlockSpec(memory_space=pltpu.VMEM)] * 5,
        out_specs=(pl.BlockSpec(memory_space=pltpu.VMEM),) * 2,
        name="side_messages",
    )(blocks, below, above, x_low, x_high)


def dotted(vector, speeds):
    running = None
    for sign_value, component in zip(vector, speeds):
        if sign_value != 0:
            if running is None:
                running = component if sign_value > 0 else -component
            else:
                running = running + component if sign_value > 0 else running - component
    return running


def equilibrium(density, speeds):
    squared = speeds[0] * speeds[0] + speeds[1] * speeds[1] + speeds[2] * speeds[2]
    baseline = 1.0 - 1.5 * squared
    weighted = {w: density * w for w in sorted(set(WEIGHTS))}
    result = [None] * 19
    result[0] = weighted[WEIGHTS[0]] * baseline
    for i in range(1, 19, 2):
        projected = dotted(VELOCITIES[i], speeds)
        even = weighted[WEIGHTS[i]] * (baseline + 4.5 * projected * projected)
        odd = weighted[WEIGHTS[i]] * (3.0 * projected)
        result[i] = even + odd
        result[i + 1] = even - odd
    return result


def inlet_values():
    squared = INLET_SPEED * INLET_SPEED
    values = []
    for weight, vector in zip(WEIGHTS, VELOCITIES):
        projected = vector[2] * INLET_SPEED
        values.append(weight * (1.0 - 1.5 * squared + 3.0 * projected + 4.5 * projected * projected))
    return values


def collided(members, kind):
    density = members[0]
    for member in members[1:]:
        density = density + member
    speeds = []
    inverse = 1.0 / density
    for axis in range(3):
        momentum = None
        for vector, member in zip(VELOCITIES, members):
            if vector[axis] != 0:
                if momentum is None:
                    momentum = member if vector[axis] > 0 else -member
                else:
                    momentum = momentum + member if vector[axis] > 0 else momentum - member
        speeds.append(momentum * inverse)
    wall = kind == 1
    inlet = kind == 2
    held = jnp.where(kind >= 2, 1.0, RELAX_RATE)
    target = jnp.where(kind >= 2, 1.0, density)
    speeds = [
        jnp.where(inlet, value, speed)
        for value, speed in zip((0.0, 0.0, INLET_SPEED), speeds)
    ]
    balanced = equilibrium(target * held, speeds)
    kept = 1.0 - held
    result = []
    for i in range(19):
        relaxed = members[i] * kept + balanced[i]
        result.append(jnp.where(wall, members[OPPOSITE[i]], relaxed))
    return result


def first_collided(density, speeds, kind):
    speeds = [jnp.where(kind == 1, -speed, speed) for speed in speeds]
    speeds = [
        jnp.where(kind == 2, value, speed)
        for value, speed in zip((0.0, 0.0, INLET_SPEED), speeds)
    ]
    density = jnp.where(kind >= 2, 1.0, density)
    return equilibrium(density, speeds)


def steps_kernel(
    blocks, below, above, x_low, x_high, y_low, y_high, kinds, out,
    native, margin, fields, old, new, rows_out, sems,
):
    lanes = lane_ids()

    for block in range(2):
        native[block, pl.ds(0, 32), :] = x_low[pl.ds(4 * block, 4)].reshape(32, 128)
        native[block, pl.ds(32, 128), :] = blocks[block]
        native[block, pl.ds(160, 32), :] = x_high[pl.ds(4 * block, 4)].reshape(32, 128)
    near = lanes % 16 < 4
    for group in range(6):
        if group == 0:
            lo, hi = x_low[8], x_low[9]
        elif group < 5:
            lo, hi = below[group - 1], above[group - 1]
        else:
            lo, hi = x_high[8], x_high[9]
        for quarter in range(4):
            column = group * 4 + quarter
            native[2, pl.ds(column * 8, 8), :] = jnp.where(
                near, roll_lanes(hi, -4 * quarter), roll_lanes(lo, 12 - 4 * quarter)
            )
    for side, message in enumerate((y_low, y_high)):
        for pair in range(3):
            value = message[pl.ds(96 + 8 * pair, 8), :]
            for quarter in range(4):
                rolled = roll_lanes(value, -4 * quarter)
                for half in range(2):
                    column = (2 * pair + half) * 4 + quarter
                    margin[side, pl.ds(column * 4, 4), :] = rolled[4 * half : 4 * half + 4]

    def put(field, third, y, value, lane, target, width):
        segment, plane = divmod(y, 8)
        target = segment * SEG + target
        value = roll_lanes(value, target - lane)
        fields[field, third, plane, :, target : target + width] = value[:, target : target + width]

    for field in range(4):
        for third in range(3):
            for half in range(2):
                for block in range(2):
                    value = native[block, pl.ds(third * 8 + half * 4 + field, 8, stride=24), :]
                    for j in range(8):
                        put(field, third, half * 8 + j + 4, value, j * 16, 4 + 16 * block, 16)
                value = native[2, pl.ds(third * 8 + half * 4 + field, 8, stride=24), :]
                for j in range(8):
                    put(field, third, half * 8 + j + 4, value, j * 16 + 12, 0, 4)
                    put(field, third, half * 8 + j + 4, value, j * 16, 36, 4)
            for side, message in enumerate((y_low, y_high)):
                value = message[pl.ds(third * 4 + field, 8, stride=12), :]
                for j in range(4):
                    y = 20 * side + j
                    put(field, third, y, value, j * 16, 4, 16)
                    put(field, third, y, value, 64 + j * 16, 20, 16)
                value = margin[side, pl.ds(third * 4 + field, 8, stride=12), :]
                for j in range(4):
                    y = 20 * side + j
                    put(field, third, y, value, j * 16, 0, 4)
                    put(field, third, y, value, 64 + j * 16, 36, 4)

    def ghosts(ref):
        for i, vector in enumerate(VELOCITIES):
            for third in range(3):
                if vector[1] > 0:
                    ref[i, third, 0] = roll_lanes(ref[i, third, 8], SEG)
                if vector[1] < 0:
                    ref[i, third, 9] = roll_lanes(ref[i, third, 1], -SEG)

    def streamed(ref, i, third, plane, lane_shift):
        vector = VELOCITIES[i]
        source = third - vector[0]
        value = ref[i, source % 3, plane + 1 - vector[1]]
        if source < 0:
            value = roll_rows(value, 1)
        elif source > 2:
            value = roll_rows(value, -1)
        return roll_lanes(value, vector[2] + lane_shift)

    def start_plane(plane, carry):
        for third in range(3):
            values = [fields[field, third, plane] for field in range(4)]
            result = first_collided(values[0], values[1:], kinds[third, plane])
            for i in range(19):
                old[i, third, plane + 1] = result[i]
        return carry

    lax.fori_loop(0, 8, start_plane, 0)
    ghosts(old)

    source, target = old, new
    for _ in range(STEPS - 1):

        def step_plane(plane, carry, source=source, target=target):
            for third in range(3):
                members = [streamed(source, i, third, plane, 0) for i in range(19)]
                result = collided(members, kinds[third, plane])
                for i in range(19):
                    target[i, third, plane + 1] = result[i]
            return carry

        lax.fori_loop(0, 8, step_plane, 0)
        ghosts(target)
        source, target = target, source

    copies = []
    for i in range(19):
        for third in range(3):
            for plane in range(8):
                for segment in range(3):
                    y = segment * 8 + plane - HALO
                    if 0 <= y < 16:
                        value = streamed(source, i, third, plane, -(segment * SEG + HALO))
                        rows_out[i, pl.ds(third * 16 + y, 8, stride=48), :] = value
        copy = pltpu.make_async_copy(rows_out.at[i, pl.ds(HALO * 16, 256), :], out.at[i], sems.at[i])
        copy.start()
        copies.append(copy)
    for copy in copies:
        copy.wait()


def run_steps(blocks, below, above, x_low, x_high, y_low, y_high, kinds):
    return pl.pallas_call(
        steps_kernel,
        out_shape=jax.ShapeDtypeStruct((19, 256, 128), F32),
        in_specs=[pl.BlockSpec(memory_space=pltpu.VMEM)] * 8,
        out_specs=pl.BlockSpec(memory_space=pl.ANY),
        scratch_shapes=[
            pltpu.VMEM((3, 192, 128), F32),
            pltpu.VMEM((2, 96, 128), F32),
            pltpu.VMEM((4, 3, 8, 8, 128), F32),
            pltpu.VMEM((19, 3, 10, 8, 128), F32),
            pltpu.VMEM((19, 3, 10, 8, 128), F32),
            pltpu.VMEM((19, 384, 128), F32),
            pltpu.SemaphoreType.DMA((19,)),
        ],
        name="run_steps",
    )(blocks, below, above, x_low, x_high, y_low, y_high, kinds)


def margin_of(array, axis, dim):
    length = array.shape[dim]
    last = lax.slice_in_dim(array, length - HALO, length, axis=dim)
    first = lax.slice_in_dim(array, 0, HALO, axis=dim)
    return jnp.concatenate([from_before(last, axis), array, from_after(first, axis)], axis=dim)


def compute_kinds(site_kind):
    kinds = site_kind
    for dim, axis in enumerate(("gx", "gy", "ba")):
        kinds = margin_of(kinds, axis, dim)
    kinds = kinds.reshape(8, 3, 3, 8, SEG).transpose(1, 3, 0, 2, 4).reshape(3, 8, 8, 3 * SEG)
    return jnp.pad(kinds, ((0, 0), (0, 0), (0, 0), (0, 128 - 3 * SEG)))


def on_device(moved_fields, send_slot, recv_index, site_kind):
    slots = moved_fields.shape[3]
    held = moved_fields.reshape(slots, 4, 32, 128).transpose(0, 2, 1, 3).reshape(slots, 128, 128)
    outgoing = gather_blocks(send_slot.reshape(-1), held)
    arrived = lax.all_to_all(outgoing, "gy", split_axis=0, concat_axis=0, tiled=True)
    kinds = compute_kinds(site_kind)
    blocks, low, high = pick_blocks(recv_index.reshape(-1), arrived)
    below = from_before(high, "ba")
    above = from_after(low, "ba")
    by_x = blocks.reshape(2, 16, 8, 128)

    def x_slab(start):
        group = start // 4
        return jnp.concatenate(
            [
                by_x[0, start : start + 4],
                by_x[1, start : start + 4],
                below[group : group + 1],
                above[group : group + 1],
            ]
        )

    x_low = from_before(x_slab(12), "gx")
    x_high = from_after(x_slab(0), "gx")
    down, up = side_messages(blocks, below, above, x_low, x_high)
    y_low = from_before(up, "gy")
    y_high = from_after(down, "gy")
    out = run_steps(blocks, below, above, x_low, x_high, y_low, y_high, kinds)
    return out.reshape(19, 16, 16, 128)[..., :32]


def solution(mesh):
    return jax.shard_map(
        on_device,
        mesh=mesh,
        in_specs=(
            P("gx", "gy", "ba", None, None, None),
            P("gx", "gy", "ba", None, None),
            P("gx", "gy", "ba", None),
            P("gx", "gy", "ba"),
        ),
        out_specs=P(None, "gx", "gy", "ba"),
        check_vma=False,
    )
```

```python
import jax
import jax.numpy as jnp
from jax import lax
from jax.experimental import pallas as pl
from jax.experimental.pallas import tpu as pltpu
from jax.sharding import PartitionSpec as P

STEPS = 4
HALO = 4

VELOCITIES = (
    (0, 0, 0),
    (1, 0, 0),
    (-1, 0, 0),
    (0, 1, 0),
    (0, -1, 0),
    (0, 0, 1),
    (0, 0, -1),
    (1, 1, 0),
    (-1, -1, 0),
    (1, -1, 0),
    (-1, 1, 0),
    (1, 0, 1),
    (-1, 0, -1),
    (1, 0, -1),
    (-1, 0, 1),
    (0, 1, 1),
    (0, -1, -1),
    (0, 1, -1),
    (0, -1, 1),
)
WEIGHTS = (1.0 / 3.0,) + (1.0 / 18.0,) * 6 + (1.0 / 36.0,) * 12
OPPOSITE = (0, 2, 1, 4, 3, 6, 5, 8, 7, 10, 9, 12, 11, 14, 13, 16, 15, 18, 17)
RELAX_RATE = 1.25
INLET_SPEED = 0.05

SEG = 40
F32 = jnp.float32


def shifted_pairs(axis, step):
    devices = lax.axis_size(axis)
    return [(i, (i + step) % devices) for i in range(devices)]


def from_before(array, axis):
    return lax.ppermute(array, axis, shifted_pairs(axis, 1))


def from_after(array, axis):
    return lax.ppermute(array, axis, shifted_pairs(axis, -1))


def lane_ids():
    return lax.broadcasted_iota(jnp.int32, (8, 128), 1)


def row_ids():
    return lax.broadcasted_iota(jnp.int32, (8, 128), 0)


def roll_lanes(value, amount):
    amount = amount % 128
    return value if amount == 0 else pltpu.roll(value, amount, 1)


def roll_rows(value, amount):
    amount = amount % 8
    return value if amount == 0 else pltpu.roll(value, amount, 0)


RELAY = 5
FIRST_HOPS = {1: (1, 6, -4), -1: (-1, 4, -6), 2: (2, 7, -3), -2: (-2, 3, -7), 3: (8,)}
KEPT = (0, RELAY, -RELAY)
UPWARD = (3, 4, 5, 6, 7, 8)
DOWNWARD = (-7, -6, -5, -4, -3)
MARK = 8


def gather_kernel(wanted, held, *refs):
    outs, sems = refs[:-1], refs[-1]
    devices = wanted.shape[0]
    me = lax.axis_index("gy")
    copies = []
    for out, offsets in zip(outs, list(FIRST_HOPS.values()) + [KEPT]):
        for place, offset in enumerate(offsets):
            slot = wanted[lax.rem(me + offset + devices, devices)]
            target = out.at[place, pl.ds(0, 128), :]
            copy = pltpu.make_async_copy(
                held.at[jnp.maximum(slot, 0)], target, sems.at[len(copies)]
            )
            copy.start()
            copies.append(copy)
            live = jnp.where(slot >= 0, 1.0, 0.0)
            out[place, pl.ds(128, MARK), :] = jnp.full((MARK, 128), live, F32)
    for copy in copies:
        copy.wait()


def gather_blocks(wanted, held):
    sizes = [len(offsets) for offsets in FIRST_HOPS.values()] + [len(KEPT)]
    return pl.pallas_call(
        gather_kernel,
        out_shape=[jax.ShapeDtypeStruct((size, 128 + MARK, 128), F32) for size in sizes],
        in_specs=[
            pl.BlockSpec(memory_space=pltpu.SMEM),
            pl.BlockSpec(memory_space=pl.ANY),
        ],
        out_specs=[pl.BlockSpec(memory_space=pltpu.VMEM)] * len(sizes),
        scratch_shapes=[pltpu.SemaphoreType.DMA((sum(sizes),))],
        compiler_params=pltpu.CompilerParams(vmem_limit_bytes=6 << 20),
        name="gather_blocks",
    )(wanted, held)


def merge_kernel(*refs):
    sources, outs = refs[:-2], refs[-2:]
    where = {}
    for source, offsets in zip(sources, list(FIRST_HOPS.values()) + [KEPT]):
        for place, offset in enumerate(offsets):
            where[offset] = (source, place)
    for out, offsets in zip(outs, (UPWARD, DOWNWARD)):
        first, second, seen = [], [], None
        for offset in offsets:
            source, place = where[offset]
            live = source[place, pl.ds(128, MARK), :]
            before = jnp.zeros_like(live) if seen is None else seen
            first.append((live > 0.5) & (before < 0.5))
            second.append((live > 0.5) & (before > 0.5))
            seen = before + live
        for tile in range(16):
            rows = pl.ds(8 * tile, 8)
            values = [where[offset][0][where[offset][1], rows, :] for offset in offsets]
            for place, masks in enumerate((first, second)):
                result = values[0]
                for mask, value in zip(masks[1:], values[1:]):
                    result = jnp.where(mask, value, result)
                out[place, rows, :] = result


def merge_blocks(arrays):
    return pl.pallas_call(
        merge_kernel,
        out_shape=(jax.ShapeDtypeStruct((2, 128, 128), F32),) * 2,
        in_specs=[pl.BlockSpec(memory_space=pltpu.VMEM)] * len(arrays),
        out_specs=(pl.BlockSpec(memory_space=pltpu.VMEM),) * 2,
        compiler_params=pltpu.CompilerParams(vmem_limit_bytes=6 << 20),
        name="merge_blocks",
    )(*arrays)


def pick_kernel(senders, *refs):
    sources, (from_below, from_above, blocks, low, high, sems) = refs[:-6], refs[-6:]
    devices = lax.axis_size("gy")
    me = lax.axis_index("gy")
    offsets = [lax.rem(me - senders[t] + devices, devices) for t in range(2)]

    def copy_of(source, t):
        return pltpu.make_async_copy(source, blocks.at[t], sems.at[t])

    for t in range(2):
        offset, other = offsets[t], offsets[1 - t]
        for source, reached in zip(sources, list(FIRST_HOPS) + [0]):
            if reached != 3:
                pl.when(offset == reached % devices)(
                    lambda source=source, t=t: copy_of(source.at[0, pl.ds(0, 128), :], t).start()
                )
        for source, lowest, highest in (
            (from_below, UPWARD[0], UPWARD[-1]),
            (from_above, DOWNWARD[0] + devices, DOWNWARD[-1] + devices),
        ):
            place = jnp.where((other >= lowest) & (other < offset), 1, 0)
            pl.when((offset >= lowest) & (offset <= highest))(
                lambda source=source, place=place, t=t: copy_of(source.at[place], t).start()
            )
    for t in range(2):
        copy_of(from_below.at[0], t).wait()
    part = (lane_ids() % 16) // 4
    for group in range(4):
        first = None
        last = None
        for quarter in range(4):
            rows = pl.ds((group * 4 + quarter) * 8, 8)
            near = roll_lanes(blocks[0, rows, :], 4 * quarter)
            far = roll_lanes(blocks[1, rows, :], 4 * quarter - 12)
            first = near if first is None else jnp.where(part == quarter, near, first)
            last = far if last is None else jnp.where(part == quarter, far, last)
        low[group] = first
        high[group] = last


def pick_blocks(senders, arrays):
    return pl.pallas_call(
        pick_kernel,
        out_shape=(
            jax.ShapeDtypeStruct((2, 128, 128), F32),
            jax.ShapeDtypeStruct((4, 8, 128), F32),
            jax.ShapeDtypeStruct((4, 8, 128), F32),
        ),
        in_specs=[pl.BlockSpec(memory_space=pltpu.SMEM)]
        + [pl.BlockSpec(memory_space=pl.ANY)] * len(arrays),
        out_specs=(pl.BlockSpec(memory_space=pltpu.VMEM),) * 3,
        scratch_shapes=[pltpu.SemaphoreType.DMA((2,))],
        compiler_params=pltpu.CompilerParams(vmem_limit_bytes=4 << 20),
        name="pick_blocks",
    )(senders, *arrays)


def rebalanced(moved_fields, send_slot, recv_index):
    slots = moved_fields.shape[3]
    held = moved_fields.reshape(slots, 4, 32, 128).transpose(0, 2, 1, 3).reshape(slots, 128, 128)
    *messages, kept = gather_blocks(send_slot.reshape(-1), held)
    arrays = [
        lax.ppermute(message, "gy", shifted_pairs("gy", hop))
        for hop, message in zip(FIRST_HOPS, messages)
    ] + [kept]
    upward, downward = merge_blocks(arrays)
    from_below = lax.ppermute(upward, "gy", shifted_pairs("gy", RELAY))
    from_above = lax.ppermute(downward, "gy", shifted_pairs("gy", -RELAY))
    return pick_blocks(recv_index.reshape(-1), arrays + [from_below, from_above])


def row_tiles(blocks, below, above, x_low, x_high):
    entries = []
    for column in range(24):
        if column < 4:
            entries.append((x_low[column], x_low[4 + column]))
        elif column < 20:
            rows = pl.ds((column - 4) * 8, 8)
            entries.append((blocks[0, rows, :], blocks[1, rows, :]))
        else:
            entries.append((x_high[column - 20], x_high[column - 16]))
    for group in range(6):
        if group == 0:
            entries.append((x_low[8], x_low[9]))
        elif group < 5:
            entries.append((below[group - 1], above[group - 1]))
        else:
            entries.append((x_high[8], x_high[9]))
    return entries


def side_kernel(blocks, below, above, x_low, x_high, down, up):
    left = lane_ids() < 64
    top = row_ids() < 4
    entries = row_tiles(blocks, below, above, x_low, x_high)
    for pair in range(15):
        first, second = entries[2 * pair], entries[2 * pair + 1]
        a = jnp.where(left, first[0], roll_lanes(first[1], 64))
        b = jnp.where(left, second[0], roll_lanes(second[1], 64))
        down[pl.ds(8 * pair, 8), :] = jnp.where(top, a, roll_rows(b, 4))
        a = jnp.where(left, roll_lanes(first[0], 64), first[1])
        b = jnp.where(left, roll_lanes(second[0], 64), second[1])
        up[pl.ds(8 * pair, 8), :] = jnp.where(top, roll_rows(a, 4), b)


def side_messages(blocks, below, above, x_low, x_high):
    return pl.pallas_call(
        side_kernel,
        out_shape=(jax.ShapeDtypeStruct((120, 128), F32),) * 2,
        in_specs=[pl.BlockSpec(memory_space=pltpu.VMEM)] * 5,
        out_specs=(pl.BlockSpec(memory_space=pltpu.VMEM),) * 2,
        compiler_params=pltpu.CompilerParams(vmem_limit_bytes=4 << 20),
        name="side_messages",
    )(blocks, below, above, x_low, x_high)


def dotted(vector, speeds):
    running = None
    for sign_value, component in zip(vector, speeds):
        if sign_value != 0:
            if running is None:
                running = component if sign_value > 0 else -component
            else:
                running = running + component if sign_value > 0 else running - component
    return running


def equilibrium(density, speeds):
    squared = speeds[0] * speeds[0] + speeds[1] * speeds[1] + speeds[2] * speeds[2]
    baseline = 1.0 - 1.5 * squared
    weighted = {w: density * w for w in sorted(set(WEIGHTS))}
    result = [None] * 19
    result[0] = weighted[WEIGHTS[0]] * baseline
    for i in range(1, 19, 2):
        projected = dotted(VELOCITIES[i], speeds)
        even = weighted[WEIGHTS[i]] * (baseline + 4.5 * projected * projected)
        odd = weighted[WEIGHTS[i]] * (3.0 * projected)
        result[i] = even + odd
        result[i + 1] = even - odd
    return result


def collided(members, kind):
    density = members[0]
    for member in members[1:]:
        density = density + member
    speeds = []
    inverse = 1.0 / density
    for axis in range(3):
        momentum = None
        for vector, member in zip(VELOCITIES, members):
            if vector[axis] != 0:
                if momentum is None:
                    momentum = member if vector[axis] > 0 else -member
                else:
                    momentum = momentum + member if vector[axis] > 0 else momentum - member
        speeds.append(momentum * inverse)
    wall = kind == 1
    inlet = kind == 2
    held = jnp.where(kind >= 2, 1.0, RELAX_RATE)
    target = jnp.where(kind >= 2, 1.0, density)
    speeds = [
        jnp.where(inlet, value, speed)
        for value, speed in zip((0.0, 0.0, INLET_SPEED), speeds)
    ]
    balanced = equilibrium(target * held, speeds)
    kept = 1.0 - held
    result = []
    for i in range(19):
        relaxed = members[i] * kept + balanced[i]
        result.append(jnp.where(wall, members[OPPOSITE[i]], relaxed))
    return result


def first_collided(density, speeds, kind):
    speeds = [jnp.where(kind == 1, -speed, speed) for speed in speeds]
    speeds = [
        jnp.where(kind == 2, value, speed)
        for value, speed in zip((0.0, 0.0, INLET_SPEED), speeds)
    ]
    density = jnp.where(kind >= 2, 1.0, density)
    return equilibrium(density, speeds)


def steps_kernel(
    blocks, below, above, x_low, x_high, y_low, y_high, kinds, out,
    native, margin, fields, old, new, rows_out, sems,
):
    lanes = lane_ids()

    for block in range(2):
        native[block, pl.ds(0, 32), :] = x_low[pl.ds(4 * block, 4)].reshape(32, 128)
        native[block, pl.ds(32, 128), :] = blocks[block]
        native[block, pl.ds(160, 32), :] = x_high[pl.ds(4 * block, 4)].reshape(32, 128)
    near = lanes % 16 < 4
    for group in range(6):
        if group == 0:
            lo, hi = x_low[8], x_low[9]
        elif group < 5:
            lo, hi = below[group - 1], above[group - 1]
        else:
            lo, hi = x_high[8], x_high[9]
        for quarter in range(4):
            column = group * 4 + quarter
            native[2, pl.ds(column * 8, 8), :] = jnp.where(
                near, roll_lanes(hi, -4 * quarter), roll_lanes(lo, 12 - 4 * quarter)
            )
    for side, message in enumerate((y_low, y_high)):
        for pair in range(3):
            value = message[pl.ds(96 + 8 * pair, 8), :]
            for quarter in range(4):
                rolled = roll_lanes(value, -4 * quarter)
                for half in range(2):
                    column = (2 * pair + half) * 4 + quarter
                    margin[side, pl.ds(column * 4, 4), :] = rolled[4 * half : 4 * half + 4]

    def put(field, third, y, value, lane, target, width):
        segment, plane = divmod(y, 8)
        target = segment * SEG + target
        value = roll_lanes(value, target - lane)
        fields[field, third, plane, :, target : target + width] = value[:, target : target + width]

    for field in range(4):
        for third in range(3):
            for half in range(2):
                for block in range(2):
                    value = native[block, pl.ds(third * 8 + half * 4 + field, 8, stride=24), :]
                    for j in range(8):
                        put(field, third, half * 8 + j + 4, value, j * 16, 4 + 16 * block, 16)
                value = native[2, pl.ds(third * 8 + half * 4 + field, 8, stride=24), :]
                for j in range(8):
                    put(field, third, half * 8 + j + 4, value, j * 16 + 12, 0, 4)
                    put(field, third, half * 8 + j + 4, value, j * 16, 36, 4)
            for side, message in enumerate((y_low, y_high)):
                value = message[pl.ds(third * 4 + field, 8, stride=12), :]
                for j in range(4):
                    y = 20 * side + j
                    put(field, third, y, value, j * 16, 4, 16)
                    put(field, third, y, value, 64 + j * 16, 20, 16)
                value = margin[side, pl.ds(third * 4 + field, 8, stride=12), :]
                for j in range(4):
                    y = 20 * side + j
                    put(field, third, y, value, j * 16, 0, 4)
                    put(field, third, y, value, 64 + j * 16, 36, 4)

    def ghosts(ref):
        for i, vector in enumerate(VELOCITIES):
            for third in range(3):
                if vector[1] > 0:
                    ref[i, third, 0] = roll_lanes(ref[i, third, 8], SEG)
                if vector[1] < 0:
                    ref[i, third, 9] = roll_lanes(ref[i, third, 1], -SEG)

    def streamed(ref, i, third, plane, lane_shift):
        vector = VELOCITIES[i]
        source = third - vector[0]
        value = ref[i, source % 3, plane + 1 - vector[1]]
        if source < 0:
            value = roll_rows(value, 1)
        elif source > 2:
            value = roll_rows(value, -1)
        return roll_lanes(value, vector[2] + lane_shift)

    def start_plane(plane, carry):
        for third in range(3):
            values = [fields[field, third, plane] for field in range(4)]
            result = first_collided(values[0], values[1:], kinds[third, plane])
            for i in range(19):
                old[i, third, plane + 1] = result[i]
        return carry

    lax.fori_loop(0, 8, start_plane, 0)
    ghosts(old)

    source, target = old, new
    for _ in range(STEPS - 1):

        def step_plane(plane, carry, source=source, target=target):
            for third in range(3):
                members = [streamed(source, i, third, plane, 0) for i in range(19)]
                result = collided(members, kinds[third, plane])
                for i in range(19):
                    target[i, third, plane + 1] = result[i]
            return carry

        lax.fori_loop(0, 8, step_plane, 0)
        ghosts(target)
        source, target = target, source

    copies = []
    for i in range(19):
        for third in range(3):
            for plane in range(8):
                for segment in range(3):
                    y = segment * 8 + plane - HALO
                    if 0 <= y < 16:
                        value = streamed(source, i, third, plane, -(segment * SEG + HALO))
                        rows_out[i, pl.ds(third * 16 + y, 8, stride=48), :] = value
        copy = pltpu.make_async_copy(rows_out.at[i, pl.ds(HALO * 16, 256), :], out.at[i], sems.at[i])
        copy.start()
        copies.append(copy)
    for copy in copies:
        copy.wait()


def run_steps(blocks, below, above, x_low, x_high, y_low, y_high, kinds):
    return pl.pallas_call(
        steps_kernel,
        out_shape=jax.ShapeDtypeStruct((19, 256, 128), F32),
        in_specs=[pl.BlockSpec(memory_space=pltpu.VMEM)] * 8,
        out_specs=pl.BlockSpec(memory_space=pl.ANY),
        scratch_shapes=[
            pltpu.VMEM((3, 192, 128), F32),
            pltpu.VMEM((2, 96, 128), F32),
            pltpu.VMEM((4, 3, 8, 8, 128), F32),
            pltpu.VMEM((19, 3, 10, 8, 128), F32),
            pltpu.VMEM((19, 3, 10, 8, 128), F32),
            pltpu.VMEM((19, 384, 128), F32),
            pltpu.SemaphoreType.DMA((19,)),
        ],
        compiler_params=pltpu.CompilerParams(vmem_limit_bytes=20 << 20),
        name="run_steps",
    )(blocks, below, above, x_low, x_high, y_low, y_high, kinds)


def margin_of(array, axis, dim):
    length = array.shape[dim]
    last = lax.slice_in_dim(array, length - HALO, length, axis=dim)
    first = lax.slice_in_dim(array, 0, HALO, axis=dim)
    return jnp.concatenate([from_before(last, axis), array, from_after(first, axis)], axis=dim)


def compute_kinds(site_kind):
    kinds = site_kind
    for dim, axis in ((0, "gx"), (2, "ba"), (1, "gy")):
        kinds = margin_of(kinds, axis, dim)
    kinds = kinds.reshape(8, 3, 3, 8, SEG).transpose(1, 3, 0, 2, 4).reshape(3, 8, 8, 3 * SEG)
    return jnp.pad(kinds, ((0, 0), (0, 0), (0, 0), (0, 128 - 3 * SEG)))


def on_device(moved_fields, send_slot, recv_index, site_kind):
    kinds = compute_kinds(site_kind)
    blocks, low, high = rebalanced(moved_fields, send_slot, recv_index)
    below = from_before(high, "ba")
    above = from_after(low, "ba")
    by_x = blocks.reshape(2, 16, 8, 128)

    def x_slab(start):
        group = start // 4
        return jnp.concatenate(
            [
                by_x[0, start : start + 4],
                by_x[1, start : start + 4],
                below[group : group + 1],
                above[group : group + 1],
            ]
        )

    x_low = from_before(x_slab(12), "gx")
    x_high = from_after(x_slab(0), "gx")
    down, up = side_messages(blocks, below, above, x_low, x_high)
    y_low = from_before(up, "gy")
    y_high = from_after(down, "gy")
    out = run_steps(blocks, below, above, x_low, x_high, y_low, y_high, kinds)
    return out.reshape(19, 16, 16, 128)[..., :32]


def solution(mesh):
    return jax.shard_map(
        on_device,
        mesh=mesh,
        in_specs=(
            P("gx", "gy", "ba", None, None, None),
            P("gx", "gy", "ba", None, None),
            P("gx", "gy", "ba", None),
            P("gx", "gy", "ba"),
        ),
        out_specs=P(None, "gx", "gy", "ba"),
        check_vma=False,
    )
```

```python
import jax
import jax.numpy as jnp
from jax import lax
from jax.experimental import pallas as pl
from jax.experimental.pallas import tpu as pltpu
from jax.sharding import PartitionSpec as P

STEPS = 4
HALO = 4

VELOCITIES = (
    (0, 0, 0),
    (1, 0, 0),
    (-1, 0, 0),
    (0, 1, 0),
    (0, -1, 0),
    (0, 0, 1),
    (0, 0, -1),
    (1, 1, 0),
    (-1, -1, 0),
    (1, -1, 0),
    (-1, 1, 0),
    (1, 0, 1),
    (-1, 0, -1),
    (1, 0, -1),
    (-1, 0, 1),
    (0, 1, 1),
    (0, -1, -1),
    (0, 1, -1),
    (0, -1, 1),
)
WEIGHTS = (1.0 / 3.0,) + (1.0 / 18.0,) * 6 + (1.0 / 36.0,) * 12
OPPOSITE = (0, 2, 1, 4, 3, 6, 5, 8, 7, 10, 9, 12, 11, 14, 13, 16, 15, 18, 17)
RELAX_RATE = 1.25
INLET_SPEED = 0.05

SEG = 40
F32 = jnp.float32


def shifted_pairs(axis, step):
    devices = lax.axis_size(axis)
    return [(i, (i + step) % devices) for i in range(devices)]


def from_before(array, axis):
    return lax.ppermute(array, axis, shifted_pairs(axis, 1))


def from_after(array, axis):
    return lax.ppermute(array, axis, shifted_pairs(axis, -1))


def lane_ids():
    return lax.broadcasted_iota(jnp.int32, (8, 128), 1)


def row_ids():
    return lax.broadcasted_iota(jnp.int32, (8, 128), 0)


def roll_lanes(value, amount):
    amount = amount % 128
    return value if amount == 0 else pltpu.roll(value, amount, 1)


def kind_rows(third, plane):
    return pl.ds((third * 8 + plane) * 8, 8)


def column_rows(column):
    return pl.ds((column % 3) * 64 + column // 3, 8, stride=8)


def roll_rows(value, amount):
    amount = amount % 8
    return value if amount == 0 else pltpu.roll(value, amount, 0)


RELAY = 5
FIRST_HOPS = {1: (1, 6, -4), -1: (-1, 4, -6), 2: (2, 7, -3), -2: (-2, 3, -7), 3: (8,)}
KEPT = (0, RELAY, -RELAY)
UPWARD = (3, 4, 5, 6, 7, 8)
DOWNWARD = (-7, -6, -5, -4, -3)
MARK = 8


def gather_kernel(wanted, held, *refs):
    outs, sems = refs[:-1], refs[-1]
    devices = wanted.shape[0]
    me = lax.axis_index("gy")
    copies = []
    for out, offsets in zip(outs, list(FIRST_HOPS.values()) + [KEPT]):
        for place, offset in enumerate(offsets):
            slot = wanted[lax.rem(me + offset + devices, devices)]
            target = out.at[place, pl.ds(0, 128), :]
            copy = pltpu.make_async_copy(
                held.at[jnp.maximum(slot, 0)], target, sems.at[len(copies)]
            )
            copy.start()
            copies.append(copy)
            live = jnp.where(slot >= 0, 1.0, 0.0)
            out[place, pl.ds(128, MARK), :] = jnp.full((MARK, 128), live, F32)
    for copy in copies:
        copy.wait()


def gather_blocks(wanted, held):
    sizes = [len(offsets) for offsets in FIRST_HOPS.values()] + [len(KEPT)]
    return pl.pallas_call(
        gather_kernel,
        out_shape=[jax.ShapeDtypeStruct((size, 128 + MARK, 128), F32) for size in sizes],
        in_specs=[
            pl.BlockSpec(memory_space=pltpu.SMEM),
            pl.BlockSpec(memory_space=pltpu.HBM),
        ],
        out_specs=[pl.BlockSpec(memory_space=pltpu.VMEM)] * len(sizes),
        scratch_shapes=[pltpu.SemaphoreType.DMA((sum(sizes),))],
        compiler_params=pltpu.CompilerParams(vmem_limit_bytes=6 << 20),
        name="gather_blocks",
    )(wanted, held)


def merge_kernel(*refs):
    sources, outs = refs[:-2], refs[-2:]
    where = {}
    for source, offsets in zip(sources, list(FIRST_HOPS.values()) + [KEPT]):
        for place, offset in enumerate(offsets):
            where[offset] = (source, place)
    for out, offsets in zip(outs, (UPWARD, DOWNWARD)):
        first, second, seen = [], [], None
        for offset in offsets:
            source, place = where[offset]
            live = source[place, pl.ds(128, MARK), :]
            before = jnp.zeros_like(live) if seen is None else seen
            first.append((live > 0.5) & (before < 0.5))
            second.append((live > 0.5) & (before > 0.5))
            seen = before + live
        for tile in range(16):
            rows = pl.ds(8 * tile, 8)
            values = [where[offset][0][where[offset][1], rows, :] for offset in offsets]
            for place, masks in enumerate((first, second)):
                result = values[0]
                for mask, value in zip(masks[1:], values[1:]):
                    result = jnp.where(mask, value, result)
                out[place, rows, :] = result


def merge_blocks(arrays):
    return pl.pallas_call(
        merge_kernel,
        out_shape=(jax.ShapeDtypeStruct((2, 128, 128), F32),) * 2,
        in_specs=[pl.BlockSpec(memory_space=pltpu.VMEM)] * len(arrays),
        out_specs=(pl.BlockSpec(memory_space=pltpu.VMEM),) * 2,
        compiler_params=pltpu.CompilerParams(vmem_limit_bytes=6 << 20),
        name="merge_blocks",
    )(*arrays)


def pick_kernel(senders, kinds, *refs):
    sources, (from_below, from_above, blocks, low, high, sems) = refs[:-6], refs[-6:]
    devices = lax.axis_size("gy")
    me = lax.axis_index("gy")
    offsets = [lax.rem(me - senders[t] + devices, devices) for t in range(2)]

    def copy_of(source, t):
        return pltpu.make_async_copy(source, blocks.at[t], sems.at[t])

    for t in range(2):
        offset, other = offsets[t], offsets[1 - t]
        for source, reached in zip(sources, list(FIRST_HOPS) + [0]):
            if reached != 3:
                pl.when(offset == reached % devices)(
                    lambda source=source, t=t: copy_of(source.at[0, pl.ds(0, 128), :], t).start()
                )
        for source, lowest, highest in (
            (from_below, UPWARD[0], UPWARD[-1]),
            (from_above, DOWNWARD[0] + devices, DOWNWARD[-1] + devices),
        ):
            place = jnp.where((other >= lowest) & (other < offset), 1, 0)
            pl.when((offset >= lowest) & (offset <= highest))(
                lambda source=source, place=place, t=t: copy_of(source.at[place], t).start()
            )
    for t in range(2):
        copy_of(from_below.at[0], t).wait()
    part = (lane_ids() % 16) // 4
    for group in range(4):
        first = None
        last = None
        for quarter in range(4):
            rows = pl.ds((group * 4 + quarter) * 8, 8)
            near = roll_lanes(blocks[0, rows, :], 4 * quarter)
            far = roll_lanes(blocks[1, rows, :], 4 * quarter - 12)
            first = near if first is None else jnp.where(part == quarter, near, first)
            last = far if last is None else jnp.where(part == quarter, far, last)
        low[group] = first
        high[group] = last
    part = (lane_ids() % SEG) // 4
    for third in range(3):
        first = None
        last = None
        for plane in range(8):
            value = kinds[kind_rows(third, plane), :]
            near = roll_lanes(value, 4 * plane - 4)
            far = roll_lanes(value, 4 * plane - 32)
            first = near if first is None else jnp.where(part == plane, near, first)
            last = far if last is None else jnp.where(part == plane, far, last)
        low[4 + third] = first
        high[4 + third] = last


def pick_blocks(senders, kinds, arrays):
    return pl.pallas_call(
        pick_kernel,
        out_shape=(
            jax.ShapeDtypeStruct((2, 128, 128), F32),
            jax.ShapeDtypeStruct((7, 8, 128), F32),
            jax.ShapeDtypeStruct((7, 8, 128), F32),
        ),
        in_specs=[
            pl.BlockSpec(memory_space=pltpu.SMEM),
            pl.BlockSpec(memory_space=pltpu.VMEM),
        ]
        + [pl.BlockSpec(memory_space=pl.ANY)] * len(arrays),
        out_specs=(pl.BlockSpec(memory_space=pltpu.VMEM),) * 3,
        scratch_shapes=[pltpu.SemaphoreType.DMA((2,))],
        compiler_params=pltpu.CompilerParams(vmem_limit_bytes=4 << 20),
        name="pick_blocks",
    )(senders, kinds, *arrays)


def rebalanced(moved_fields, send_slot, recv_index, kinds):
    slots = moved_fields.shape[3]
    held = moved_fields.reshape(slots, 4, 32, 128).transpose(0, 2, 1, 3).reshape(slots, 128, 128)
    *messages, kept = gather_blocks(send_slot.reshape(-1), held)
    arrays = [
        lax.ppermute(message, "gy", shifted_pairs("gy", hop))
        for hop, message in zip(FIRST_HOPS, messages)
    ] + [kept]
    upward, downward = merge_blocks(arrays)
    from_below = lax.ppermute(upward, "gy", shifted_pairs("gy", RELAY))
    from_above = lax.ppermute(downward, "gy", shifted_pairs("gy", -RELAY))
    return pick_blocks(recv_index.reshape(-1), kinds, arrays + [from_below, from_above])


def cross_kernel(blocks, below, above, kinds, full, down, up):
    place = lane_ids() % SEG
    for third in range(3):
        for plane in range(8):
            value = kinds[kind_rows(third, plane), :]
            value = jnp.where(place < 4, roll_lanes(below[4 + third], -4 * plane), value)
            value = jnp.where(place >= 36, roll_lanes(above[4 + third], 36 - 4 * plane), value)
            full[kind_rows(third, plane), :] = value
    for message, start in ((down, 0), (up, 12)):
        for column in range(4):
            rows = pl.ds((start + column) * 8, 8)
            message[column] = blocks[0, rows, :]
            message[4 + column] = blocks[1, rows, :]
            message[10 + column] = full[column_rows(start + column + HALO), :]
        message[8] = below[start // 4]
        message[9] = above[start // 4]


def cross_messages(blocks, below, above, kinds):
    return pl.pallas_call(
        cross_kernel,
        out_shape=(
            jax.ShapeDtypeStruct((192, 128), F32),
            jax.ShapeDtypeStruct((14, 8, 128), F32),
            jax.ShapeDtypeStruct((14, 8, 128), F32),
        ),
        in_specs=[pl.BlockSpec(memory_space=pltpu.VMEM)] * 4,
        out_specs=(pl.BlockSpec(memory_space=pltpu.VMEM),) * 3,
        compiler_params=pltpu.CompilerParams(vmem_limit_bytes=4 << 20),
        name="cross_messages",
    )(blocks, below, above, kinds)


def row_tiles(blocks, below, above, x_low, x_high):
    entries = []
    for column in range(24):
        if column < 4:
            entries.append((x_low[column], x_low[4 + column]))
        elif column < 20:
            rows = pl.ds((column - 4) * 8, 8)
            entries.append((blocks[0, rows, :], blocks[1, rows, :]))
        else:
            entries.append((x_high[column - 20], x_high[column - 16]))
    for group in range(6):
        if group == 0:
            entries.append((x_low[8], x_low[9]))
        elif group < 5:
            entries.append((below[group - 1], above[group - 1]))
        else:
            entries.append((x_high[8], x_high[9]))
    return entries


def side_kernel(blocks, below, above, x_low, x_high, kinds, full, down, up):
    full[...] = kinds[...]
    for column in range(4):
        full[column_rows(column), :] = x_low[10 + column]
        full[column_rows(20 + column), :] = x_high[10 + column]
    third_of = lane_ids() // SEG
    for y in range(4):
        for message, plane, segment in ((down, y + 4, 0), (up, y, 2)):
            packed = None
            for third in range(3):
                value = roll_lanes(full[kind_rows(third, plane), :], (third - segment) * SEG)
                packed = value if packed is None else jnp.where(third_of == third, value, packed)
            message[pl.ds(120 + 8 * y, 8), :] = packed
    left = lane_ids() < 64
    top = row_ids() < 4
    entries = row_tiles(blocks, below, above, x_low, x_high)
    for pair in range(15):
        first, second = entries[2 * pair], entries[2 * pair + 1]
        a = jnp.where(left, first[0], roll_lanes(first[1], 64))
        b = jnp.where(left, second[0], roll_lanes(second[1], 64))
        down[pl.ds(8 * pair, 8), :] = jnp.where(top, a, roll_rows(b, 4))
        a = jnp.where(left, roll_lanes(first[0], 64), first[1])
        b = jnp.where(left, roll_lanes(second[0], 64), second[1])
        up[pl.ds(8 * pair, 8), :] = jnp.where(top, roll_rows(a, 4), b)


def side_messages(blocks, below, above, x_low, x_high, kinds):
    return pl.pallas_call(
        side_kernel,
        out_shape=(
            jax.ShapeDtypeStruct((192, 128), F32),
            jax.ShapeDtypeStruct((152, 128), F32),
            jax.ShapeDtypeStruct((152, 128), F32),
        ),
        in_specs=[pl.BlockSpec(memory_space=pltpu.VMEM)] * 6,
        out_specs=(pl.BlockSpec(memory_space=pltpu.VMEM),) * 3,
        compiler_params=pltpu.CompilerParams(vmem_limit_bytes=4 << 20),
        name="side_messages",
    )(blocks, below, above, x_low, x_high, kinds)


def dotted(vector, speeds):
    running = None
    for sign_value, component in zip(vector, speeds):
        if sign_value != 0:
            if running is None:
                running = component if sign_value > 0 else -component
            else:
                running = running + component if sign_value > 0 else running - component
    return running


def equilibrium(density, speeds):
    squared = speeds[0] * speeds[0] + speeds[1] * speeds[1] + speeds[2] * speeds[2]
    baseline = 1.0 - 1.5 * squared
    weighted = {w: density * w for w in sorted(set(WEIGHTS))}
    result = [None] * 19
    result[0] = weighted[WEIGHTS[0]] * baseline
    for i in range(1, 19, 2):
        projected = dotted(VELOCITIES[i], speeds)
        even = weighted[WEIGHTS[i]] * (baseline + 4.5 * projected * projected)
        odd = weighted[WEIGHTS[i]] * (3.0 * projected)
        result[i] = even + odd
        result[i + 1] = even - odd
    return result


def collided(members, kind):
    density = members[0]
    for member in members[1:]:
        density = density + member
    speeds = []
    inverse = 1.0 / density
    for axis in range(3):
        momentum = None
        for vector, member in zip(VELOCITIES, members):
            if vector[axis] != 0:
                if momentum is None:
                    momentum = member if vector[axis] > 0 else -member
                else:
                    momentum = momentum + member if vector[axis] > 0 else momentum - member
        speeds.append(momentum * inverse)
    wall = kind == 1
    inlet = kind == 2
    held = jnp.where(kind >= 2, 1.0, RELAX_RATE)
    target = jnp.where(kind >= 2, 1.0, density)
    speeds = [
        jnp.where(inlet, value, speed)
        for value, speed in zip((0.0, 0.0, INLET_SPEED), speeds)
    ]
    balanced = equilibrium(target * held, speeds)
    kept = 1.0 - held
    result = []
    for i in range(19):
        relaxed = members[i] * kept + balanced[i]
        result.append(jnp.where(wall, members[OPPOSITE[i]], relaxed))
    return result


def first_collided(density, speeds, kind):
    speeds = [jnp.where(kind == 1, -speed, speed) for speed in speeds]
    speeds = [
        jnp.where(kind == 2, value, speed)
        for value, speed in zip((0.0, 0.0, INLET_SPEED), speeds)
    ]
    density = jnp.where(kind >= 2, 1.0, density)
    return equilibrium(density, speeds)


def steps_kernel(
    blocks, below, above, x_low, x_high, y_low, y_high, near_kinds, out,
    native, margin, fields, kinds, old, new, rows_out, sems,
):
    lanes = lane_ids()

    for third in range(3):
        for plane in range(8):
            value = near_kinds[kind_rows(third, plane), :]
            if plane < 4:
                side = roll_lanes(y_low[pl.ds(120 + 8 * plane, 8), :], -third * SEG)
                value = jnp.where(lanes < SEG, side, value)
            else:
                side = roll_lanes(y_high[pl.ds(88 + 8 * plane, 8), :], (2 - third) * SEG)
                value = jnp.where(lanes >= 2 * SEG, side, value)
            kinds[third, plane] = value

    for block in range(2):
        native[block, pl.ds(0, 32), :] = x_low[pl.ds(4 * block, 4)].reshape(32, 128)
        native[block, pl.ds(32, 128), :] = blocks[block]
        native[block, pl.ds(160, 32), :] = x_high[pl.ds(4 * block, 4)].reshape(32, 128)
    near = lanes % 16 < 4
    for group in range(6):
        if group == 0:
            lo, hi = x_low[8], x_low[9]
        elif group < 5:
            lo, hi = below[group - 1], above[group - 1]
        else:
            lo, hi = x_high[8], x_high[9]
        for quarter in range(4):
            column = group * 4 + quarter
            native[2, pl.ds(column * 8, 8), :] = jnp.where(
                near, roll_lanes(hi, -4 * quarter), roll_lanes(lo, 12 - 4 * quarter)
            )
    for side, message in enumerate((y_low, y_high)):
        for pair in range(3):
            value = message[pl.ds(96 + 8 * pair, 8), :]
            for quarter in range(4):
                rolled = roll_lanes(value, -4 * quarter)
                for half in range(2):
                    column = (2 * pair + half) * 4 + quarter
                    margin[side, pl.ds(column * 4, 4), :] = rolled[4 * half : 4 * half + 4]

    def put(field, third, y, value, lane, target, width):
        segment, plane = divmod(y, 8)
        target = segment * SEG + target
        value = roll_lanes(value, target - lane)
        fields[field, third, plane, :, target : target + width] = value[:, target : target + width]

    for field in range(4):
        for third in range(3):
            for half in range(2):
                for block in range(2):
                    value = native[block, pl.ds(third * 8 + half * 4 + field, 8, stride=24), :]
                    for j in range(8):
                        put(field, third, half * 8 + j + 4, value, j * 16, 4 + 16 * block, 16)
                value = native[2, pl.ds(third * 8 + half * 4 + field, 8, stride=24), :]
                for j in range(8):
                    put(field, third, half * 8 + j + 4, value, j * 16 + 12, 0, 4)
                    put(field, third, half * 8 + j + 4, value, j * 16, 36, 4)
            for side, message in enumerate((y_low, y_high)):
                value = message[pl.ds(third * 4 + field, 8, stride=12), :]
                for j in range(4):
                    y = 20 * side + j
                    put(field, third, y, value, j * 16, 4, 16)
                    put(field, third, y, value, 64 + j * 16, 20, 16)
                value = margin[side, pl.ds(third * 4 + field, 8, stride=12), :]
                for j in range(4):
                    y = 20 * side + j
                    put(field, third, y, value, j * 16, 0, 4)
                    put(field, third, y, value, 64 + j * 16, 36, 4)

    def ghosts(ref):
        for i, vector in enumerate(VELOCITIES):
            for third in range(3):
                if vector[1] > 0:
                    ref[i, third, 0] = roll_lanes(ref[i, third, 8], SEG)
                if vector[1] < 0:
                    ref[i, third, 9] = roll_lanes(ref[i, third, 1], -SEG)

    def streamed(ref, i, third, plane, lane_shift):
        vector = VELOCITIES[i]
        source = third - vector[0]
        value = ref[i, source % 3, plane + 1 - vector[1]]
        if source < 0:
            value = roll_rows(value, 1)
        elif source > 2:
            value = roll_rows(value, -1)
        return roll_lanes(value, vector[2] + lane_shift)

    def start_plane(plane, carry):
        for third in range(3):
            values = [fields[field, third, plane] for field in range(4)]
            result = first_collided(values[0], values[1:], kinds[third, plane])
            for i in range(19):
                old[i, third, plane + 1] = result[i]
        return carry

    lax.fori_loop(0, 8, start_plane, 0)
    ghosts(old)

    source, target = old, new
    for _ in range(STEPS - 1):

        def step_plane(plane, carry, source=source, target=target):
            for third in range(3):
                members = [streamed(source, i, third, plane, 0) for i in range(19)]
                result = collided(members, kinds[third, plane])
                for i in range(19):
                    target[i, third, plane + 1] = result[i]
            return carry

        lax.fori_loop(0, 8, step_plane, 0)
        ghosts(target)
        source, target = target, source

    copies = []
    for i in range(19):
        for third in range(3):
            for plane in range(8):
                for segment in range(3):
                    y = segment * 8 + plane - HALO
                    if 0 <= y < 16:
                        value = streamed(source, i, third, plane, -(segment * SEG + HALO))
                        rows_out[i, pl.ds(third * 16 + y, 8, stride=48), :] = value
        copy = pltpu.make_async_copy(rows_out.at[i, pl.ds(HALO * 16, 256), :], out.at[i], sems.at[i])
        copy.start()
        copies.append(copy)
    for copy in copies:
        copy.wait()


def run_steps(blocks, below, above, x_low, x_high, y_low, y_high, kinds):
    return pl.pallas_call(
        steps_kernel,
        out_shape=jax.ShapeDtypeStruct((19, 256, 128), F32),
        in_specs=[pl.BlockSpec(memory_space=pltpu.VMEM)] * 8,
        out_specs=pl.BlockSpec(memory_space=pl.ANY),
        scratch_shapes=[
            pltpu.VMEM((3, 192, 128), F32),
            pltpu.VMEM((2, 96, 128), F32),
            pltpu.VMEM((4, 3, 8, 8, 128), F32),
            pltpu.VMEM((3, 8, 8, 128), F32),
            pltpu.VMEM((19, 3, 10, 8, 128), F32),
            pltpu.VMEM((19, 3, 10, 8, 128), F32),
            pltpu.VMEM((19, 384, 128), F32),
            pltpu.SemaphoreType.DMA((19,)),
        ],
        compiler_params=pltpu.CompilerParams(vmem_limit_bytes=20 << 20),
        name="run_steps",
    )(blocks, below, above, x_low, x_high, y_low, y_high, kinds)


def own_kinds(site_kind):
    kinds = jnp.pad(site_kind.astype(F32), HALO)
    kinds = kinds.reshape(8, 3, 3, 8, SEG).transpose(1, 3, 0, 2, 4).reshape(192, 3 * SEG)
    return jnp.pad(kinds, ((0, 0), (0, 128 - 3 * SEG)))


def on_device(moved_fields, send_slot, recv_index, site_kind):
    kinds = own_kinds(site_kind)
    blocks, low, high = rebalanced(moved_fields, send_slot, recv_index, kinds)
    below = from_before(high, "ba")
    above = from_after(low, "ba")
    kinds, down, up = cross_messages(blocks, below, above, kinds)
    x_low = from_before(up, "gx")
    x_high = from_after(down, "gx")
    kinds, down, up = side_messages(blocks, below, above, x_low, x_high, kinds)
    y_low = from_before(up, "gy")
    y_high = from_after(down, "gy")
    out = run_steps(blocks, below, above, x_low, x_high, y_low, y_high, kinds)
    return out.reshape(19, 16, 16, 128)[..., :32]


def solution(mesh):
    return jax.shard_map(
        on_device,
        mesh=mesh,
        in_specs=(
            P("gx", "gy", "ba", None, None, None),
            P("gx", "gy", "ba", None, None),
            P("gx", "gy", "ba", None),
            P("gx", "gy", "ba"),
        ),
        out_specs=P(None, "gx", "gy", "ba"),
        check_vma=False,
    )
```

```python
import jax
import jax.numpy as jnp
from jax import lax
from jax.experimental import pallas as pl
from jax.experimental.pallas import tpu as pltpu
from jax.sharding import PartitionSpec as P

STEPS = 4
HALO = 4

VELOCITIES = (
    (0, 0, 0),
    (1, 0, 0),
    (-1, 0, 0),
    (0, 1, 0),
    (0, -1, 0),
    (0, 0, 1),
    (0, 0, -1),
    (1, 1, 0),
    (-1, -1, 0),
    (1, -1, 0),
    (-1, 1, 0),
    (1, 0, 1),
    (-1, 0, -1),
    (1, 0, -1),
    (-1, 0, 1),
    (0, 1, 1),
    (0, -1, -1),
    (0, 1, -1),
    (0, -1, 1),
)
WEIGHTS = (1.0 / 3.0,) + (1.0 / 18.0,) * 6 + (1.0 / 36.0,) * 12
OPPOSITE = (0, 2, 1, 4, 3, 6, 5, 8, 7, 10, 9, 12, 11, 14, 13, 16, 15, 18, 17)
RELAX_RATE = 1.25
INLET_SPEED = 0.05

SEG = 40
F32 = jnp.float32


def shifted_pairs(axis, step):
    devices = lax.axis_size(axis)
    return [(i, (i + step) % devices) for i in range(devices)]


def from_before(array, axis):
    return lax.ppermute(array, axis, shifted_pairs(axis, 1))


def from_after(array, axis):
    return lax.ppermute(array, axis, shifted_pairs(axis, -1))


def lane_ids():
    return lax.broadcasted_iota(jnp.int32, (8, 128), 1)


def row_ids():
    return lax.broadcasted_iota(jnp.int32, (8, 128), 0)


def roll_lanes(value, amount):
    amount = amount % 128
    return value if amount == 0 else pltpu.roll(value, amount, 1)


def kind_rows(third, plane):
    return pl.ds((third * 8 + plane) * 8, 8)


def column_rows(column):
    return pl.ds((column % 3) * 64 + column // 3, 8, stride=8)


def roll_rows(value, amount):
    amount = amount % 8
    return value if amount == 0 else pltpu.roll(value, amount, 0)


RELAY = 5
FIRST_HOPS = {1: (1, 6, -4), -1: (-1, 4, -6), 2: (2, 7, -3), -2: (-2, 3, -7), 3: (8,)}
KEPT = (0, RELAY, -RELAY)
UPWARD = (3, 4, 5, 6, 7, 8)
DOWNWARD = (-7, -6, -5, -4, -3)


def tiles():
    return [pl.ds(8 * tile, 8) for tile in range(16)]


def gather_kernel(wanted, held, *outs):
    devices = wanted.shape[0]
    me = lax.axis_index("gy")
    for out, offsets in zip(outs, list(FIRST_HOPS.values()) + [KEPT]):
        for place, offset in enumerate(offsets):
            slot = wanted[lax.rem(me + offset + devices, devices)]
            source = jnp.maximum(slot, 0)
            for tile, rows in enumerate(tiles()):
                value = held[source, rows, :]
                if tile == 0:
                    value = jnp.where(slot >= 0, value, 0.0)
                out[place, rows, :] = value


def gather_blocks(wanted, held):
    sizes = [len(offsets) for offsets in FIRST_HOPS.values()] + [len(KEPT)]
    return pl.pallas_call(
        gather_kernel,
        out_shape=[jax.ShapeDtypeStruct((size, 128, 128), F32) for size in sizes],
        in_specs=[
            pl.BlockSpec(memory_space=pltpu.SMEM),
            pl.BlockSpec(memory_space=pltpu.VMEM),
        ],
        out_specs=[pl.BlockSpec(memory_space=pltpu.VMEM)] * len(sizes),
        compiler_params=pltpu.CompilerParams(vmem_limit_bytes=6 << 20),
        name="gather_blocks",
    )(wanted, held)


def merge_kernel(*refs):
    sources, outs = refs[:-2], refs[-2:]
    where = {}
    for source, offsets in zip(sources, list(FIRST_HOPS.values()) + [KEPT]):
        for place, offset in enumerate(offsets):
            where[offset] = (source, place)
    for out, offsets in zip(outs, (UPWARD, DOWNWARD)):
        first, second, seen = [], [], None
        for offset in offsets:
            source, place = where[offset]
            live = jnp.broadcast_to(source[place, pl.ds(0, 1), :], (8, 128)) > 0.3
            count = jnp.where(live, 1, 0)
            before = jnp.zeros_like(count) if seen is None else seen
            first.append(live & (before == 0))
            second.append(live & (before == 1))
            seen = before + count
        for rows in tiles():
            values = [where[offset][0][where[offset][1], rows, :] for offset in offsets]
            for place, masks in enumerate((first, second)):
                result = values[0]
                for mask, value in zip(masks[1:], values[1:]):
                    result = jnp.where(mask, value, result)
                out[place, rows, :] = result


def merge_blocks(arrays):
    return pl.pallas_call(
        merge_kernel,
        out_shape=(jax.ShapeDtypeStruct((2, 128, 128), F32),) * 2,
        in_specs=[pl.BlockSpec(memory_space=pltpu.VMEM)] * len(arrays),
        out_specs=(pl.BlockSpec(memory_space=pltpu.VMEM),) * 2,
        compiler_params=pltpu.CompilerParams(vmem_limit_bytes=6 << 20),
        name="merge_blocks",
    )(*arrays)


def pick_kernel(senders, kinds, *refs):
    sources, (from_below, from_above, blocks, low, high) = refs[:-5], refs[-5:]
    devices = lax.axis_size("gy")
    me = lax.axis_index("gy")
    offsets = [lax.rem(me - senders[t] + devices, devices) for t in range(2)]

    def take(condition, source, place, t):
        @pl.when(condition)
        def _():
            for rows in tiles():
                blocks[t, rows, :] = source[place, rows, :]

    for t in range(2):
        offset, other = offsets[t], offsets[1 - t]
        for source, reached in zip(sources, list(FIRST_HOPS) + [0]):
            if reached != 3:
                take(offset == reached % devices, source, 0, t)
        for source, lowest, highest in (
            (from_below, UPWARD[0], UPWARD[-1]),
            (from_above, DOWNWARD[0] + devices, DOWNWARD[-1] + devices),
        ):
            place = jnp.where((other >= lowest) & (other < offset), 1, 0)
            take((offset >= lowest) & (offset <= highest), source, place, t)
    part = (lane_ids() % 16) // 4
    for group in range(4):
        first = None
        last = None
        for quarter in range(4):
            rows = pl.ds((group * 4 + quarter) * 8, 8)
            near = roll_lanes(blocks[0, rows, :], 4 * quarter)
            far = roll_lanes(blocks[1, rows, :], 4 * quarter - 12)
            first = near if first is None else jnp.where(part == quarter, near, first)
            last = far if last is None else jnp.where(part == quarter, far, last)
        low[group] = first
        high[group] = last
    part = (lane_ids() % SEG) // 4
    for third in range(3):
        first = None
        last = None
        for plane in range(8):
            value = kinds[kind_rows(third, plane), :]
            near = roll_lanes(value, 4 * plane - 4)
            far = roll_lanes(value, 4 * plane - 32)
            first = near if first is None else jnp.where(part == plane, near, first)
            last = far if last is None else jnp.where(part == plane, far, last)
        low[4 + third] = first
        high[4 + third] = last


def pick_blocks(senders, kinds, arrays):
    return pl.pallas_call(
        pick_kernel,
        out_shape=(
            jax.ShapeDtypeStruct((2, 128, 128), F32),
            jax.ShapeDtypeStruct((7, 8, 128), F32),
            jax.ShapeDtypeStruct((7, 8, 128), F32),
        ),
        in_specs=[
            pl.BlockSpec(memory_space=pltpu.SMEM),
            pl.BlockSpec(memory_space=pltpu.VMEM),
        ]
        + [pl.BlockSpec(memory_space=pltpu.VMEM)] * len(arrays),
        out_specs=(pl.BlockSpec(memory_space=pltpu.VMEM),) * 3,
        compiler_params=pltpu.CompilerParams(vmem_limit_bytes=6 << 20),
        name="pick_blocks",
    )(senders, kinds, *arrays)


def rebalanced(moved_fields, send_slot, recv_index, kinds):
    slots = moved_fields.shape[3]
    held = moved_fields.reshape(slots, 4, 32, 128).transpose(0, 2, 1, 3).reshape(slots, 128, 128)
    *messages, kept = gather_blocks(send_slot.reshape(-1), held)
    arrays = [
        lax.ppermute(message, "gy", shifted_pairs("gy", hop))
        for hop, message in zip(FIRST_HOPS, messages)
    ] + [kept]
    upward, downward = merge_blocks(arrays)
    from_below = lax.ppermute(upward, "gy", shifted_pairs("gy", RELAY))
    from_above = lax.ppermute(downward, "gy", shifted_pairs("gy", -RELAY))
    return pick_blocks(recv_index.reshape(-1), kinds, arrays + [from_below, from_above])


def cross_kernel(blocks, below, above, kinds, full, down, up):
    place = lane_ids() % SEG
    for third in range(3):
        for plane in range(8):
            value = kinds[kind_rows(third, plane), :]
            value = jnp.where(place < 4, roll_lanes(below[4 + third], -4 * plane), value)
            value = jnp.where(place >= 36, roll_lanes(above[4 + third], 36 - 4 * plane), value)
            full[kind_rows(third, plane), :] = value
    for message, start in ((down, 0), (up, 12)):
        for column in range(4):
            rows = pl.ds((start + column) * 8, 8)
            message[column] = blocks[0, rows, :]
            message[4 + column] = blocks[1, rows, :]
            message[10 + column] = full[column_rows(start + column + HALO), :]
        message[8] = below[start // 4]
        message[9] = above[start // 4]


def cross_messages(blocks, below, above, kinds):
    return pl.pallas_call(
        cross_kernel,
        out_shape=(
            jax.ShapeDtypeStruct((192, 128), F32),
            jax.ShapeDtypeStruct((14, 8, 128), F32),
            jax.ShapeDtypeStruct((14, 8, 128), F32),
        ),
        in_specs=[pl.BlockSpec(memory_space=pltpu.VMEM)] * 4,
        out_specs=(pl.BlockSpec(memory_space=pltpu.VMEM),) * 3,
        compiler_params=pltpu.CompilerParams(vmem_limit_bytes=4 << 20),
        name="cross_messages",
    )(blocks, below, above, kinds)


def row_tiles(blocks, below, above, x_low, x_high):
    entries = []
    for column in range(24):
        if column < 4:
            entries.append((x_low[column], x_low[4 + column]))
        elif column < 20:
            rows = pl.ds((column - 4) * 8, 8)
            entries.append((blocks[0, rows, :], blocks[1, rows, :]))
        else:
            entries.append((x_high[column - 20], x_high[column - 16]))
    for group in range(6):
        if group == 0:
            entries.append((x_low[8], x_low[9]))
        elif group < 5:
            entries.append((below[group - 1], above[group - 1]))
        else:
            entries.append((x_high[8], x_high[9]))
    return entries


def side_kernel(blocks, below, above, x_low, x_high, kinds, full, down, up):
    full[...] = kinds[...]
    for column in range(4):
        full[column_rows(column), :] = x_low[10 + column]
        full[column_rows(20 + column), :] = x_high[10 + column]
    third_of = lane_ids() // SEG
    for y in range(4):
        for message, plane, segment in ((down, y + 4, 0), (up, y, 2)):
            packed = None
            for third in range(3):
                value = roll_lanes(full[kind_rows(third, plane), :], (third - segment) * SEG)
                packed = value if packed is None else jnp.where(third_of == third, value, packed)
            message[pl.ds(120 + 8 * y, 8), :] = packed
    left = lane_ids() < 64
    top = row_ids() < 4
    entries = row_tiles(blocks, below, above, x_low, x_high)
    for pair in range(15):
        first, second = entries[2 * pair], entries[2 * pair + 1]
        a = jnp.where(left, first[0], roll_lanes(first[1], 64))
        b = jnp.where(left, second[0], roll_lanes(second[1], 64))
        down[pl.ds(8 * pair, 8), :] = jnp.where(top, a, roll_rows(b, 4))
        a = jnp.where(left, roll_lanes(first[0], 64), first[1])
        b = jnp.where(left, roll_lanes(second[0], 64), second[1])
        up[pl.ds(8 * pair, 8), :] = jnp.where(top, roll_rows(a, 4), b)


def side_messages(blocks, below, above, x_low, x_high, kinds):
    return pl.pallas_call(
        side_kernel,
        out_shape=(
            jax.ShapeDtypeStruct((192, 128), F32),
            jax.ShapeDtypeStruct((152, 128), F32),
            jax.ShapeDtypeStruct((152, 128), F32),
        ),
        in_specs=[pl.BlockSpec(memory_space=pltpu.VMEM)] * 6,
        out_specs=(pl.BlockSpec(memory_space=pltpu.VMEM),) * 3,
        compiler_params=pltpu.CompilerParams(vmem_limit_bytes=4 << 20),
        name="side_messages",
    )(blocks, below, above, x_low, x_high, kinds)


def dotted(vector, speeds):
    running = None
    for sign_value, component in zip(vector, speeds):
        if sign_value != 0:
            if running is None:
                running = component if sign_value > 0 else -component
            else:
                running = running + component if sign_value > 0 else running - component
    return running


def equilibrium(density, speeds):
    squared = speeds[0] * speeds[0] + speeds[1] * speeds[1] + speeds[2] * speeds[2]
    baseline = 1.0 - 1.5 * squared
    weighted = {w: density * w for w in sorted(set(WEIGHTS))}
    result = [None] * 19
    result[0] = weighted[WEIGHTS[0]] * baseline
    for i in range(1, 19, 2):
        projected = dotted(VELOCITIES[i], speeds)
        even = weighted[WEIGHTS[i]] * (baseline + 4.5 * projected * projected)
        odd = weighted[WEIGHTS[i]] * (3.0 * projected)
        result[i] = even + odd
        result[i + 1] = even - odd
    return result


def collided(members, kind):
    density = members[0]
    for member in members[1:]:
        density = density + member
    speeds = []
    inverse = 1.0 / density
    for axis in range(3):
        momentum = None
        for vector, member in zip(VELOCITIES, members):
            if vector[axis] != 0:
                if momentum is None:
                    momentum = member if vector[axis] > 0 else -member
                else:
                    momentum = momentum + member if vector[axis] > 0 else momentum - member
        speeds.append(momentum * inverse)
    wall = kind == 1
    inlet = kind == 2
    held = jnp.where(kind >= 2, 1.0, RELAX_RATE)
    target = jnp.where(kind >= 2, 1.0, density)
    speeds = [
        jnp.where(inlet, value, speed)
        for value, speed in zip((0.0, 0.0, INLET_SPEED), speeds)
    ]
    balanced = equilibrium(target * held, speeds)
    kept = 1.0 - held
    result = []
    for i in range(19):
        relaxed = members[i] * kept + balanced[i]
        result.append(jnp.where(wall, members[OPPOSITE[i]], relaxed))
    return result


def first_collided(density, speeds, kind):
    speeds = [jnp.where(kind == 1, -speed, speed) for speed in speeds]
    speeds = [
        jnp.where(kind == 2, value, speed)
        for value, speed in zip((0.0, 0.0, INLET_SPEED), speeds)
    ]
    density = jnp.where(kind >= 2, 1.0, density)
    return equilibrium(density, speeds)


def put(fields, field, third, y, value, lane, target, width):
    segment, plane = divmod(y, 8)
    target = segment * SEG + target
    value = roll_lanes(value, target - lane)
    fields[field, third, plane, :, target : target + width] = value[:, target : target + width]


def unpack_kernel(blocks, below, above, x_low, x_high, fields, native):
    for block in range(2):
        native[block, pl.ds(0, 32), :] = x_low[pl.ds(4 * block, 4)].reshape(32, 128)
        native[block, pl.ds(32, 128), :] = blocks[block]
        native[block, pl.ds(160, 32), :] = x_high[pl.ds(4 * block, 4)].reshape(32, 128)
    near = lane_ids() % 16 < 4
    for group in range(6):
        if group == 0:
            lo, hi = x_low[8], x_low[9]
        elif group < 5:
            lo, hi = below[group - 1], above[group - 1]
        else:
            lo, hi = x_high[8], x_high[9]
        for quarter in range(4):
            column = group * 4 + quarter
            native[2, pl.ds(column * 8, 8), :] = jnp.where(
                near, roll_lanes(hi, -4 * quarter), roll_lanes(lo, 12 - 4 * quarter)
            )
    for field in range(4):
        for third in range(3):
            for half in range(2):
                rows = pl.ds(third * 8 + half * 4 + field, 8, stride=24)
                for block in range(2):
                    value = native[block, rows, :]
                    for j in range(8):
                        y = half * 8 + j + 4
                        put(fields, field, third, y, value, j * 16, 4 + 16 * block, 16)
                value = native[2, rows, :]
                for j in range(8):
                    y = half * 8 + j + 4
                    put(fields, field, third, y, value, j * 16 + 12, 0, 4)
                    put(fields, field, third, y, value, j * 16, 36, 4)


def unpacked(blocks, below, above, x_low, x_high):
    return pl.pallas_call(
        unpack_kernel,
        out_shape=jax.ShapeDtypeStruct((4, 3, 8, 8, 128), F32),
        in_specs=[pl.BlockSpec(memory_space=pltpu.VMEM)] * 5,
        out_specs=pl.BlockSpec(memory_space=pltpu.VMEM),
        scratch_shapes=[pltpu.VMEM((3, 192, 128), F32)],
        compiler_params=pltpu.CompilerParams(vmem_limit_bytes=4 << 20),
        cost_estimate=pl.CostEstimate(flops=2000000, bytes_accessed=4000000, transcendentals=0),
        name="unpack",
    )(blocks, below, above, x_low, x_high)


def steps_kernel(
    near_fields, y_low, y_high, near_kinds, out,
    margin, fields, kinds, old, new, rows_out, sems,
):
    lanes = lane_ids()

    for third in range(3):
        for plane in range(8):
            value = near_kinds[kind_rows(third, plane), :]
            if plane < 4:
                side = roll_lanes(y_low[pl.ds(120 + 8 * plane, 8), :], -third * SEG)
                value = jnp.where(lanes < SEG, side, value)
            else:
                side = roll_lanes(y_high[pl.ds(88 + 8 * plane, 8), :], (2 - third) * SEG)
                value = jnp.where(lanes >= 2 * SEG, side, value)
            kinds[third, plane] = value

    for side, message in enumerate((y_low, y_high)):
        for pair in range(3):
            value = message[pl.ds(96 + 8 * pair, 8), :]
            for quarter in range(4):
                rolled = roll_lanes(value, -4 * quarter)
                for half in range(2):
                    column = (2 * pair + half) * 4 + quarter
                    margin[side, pl.ds(column * 4, 4), :] = rolled[4 * half : 4 * half + 4]

    fields[...] = near_fields[...]
    for field in range(4):
        for third in range(3):
            rows = pl.ds(third * 4 + field, 8, stride=12)
            for side, message in enumerate((y_low, y_high)):
                value = message[rows, :]
                for j in range(4):
                    y = 20 * side + j
                    put(fields, field, third, y, value, j * 16, 4, 16)
                    put(fields, field, third, y, value, 64 + j * 16, 20, 16)
                value = margin[side, rows, :]
                for j in range(4):
                    y = 20 * side + j
                    put(fields, field, third, y, value, j * 16, 0, 4)
                    put(fields, field, third, y, value, 64 + j * 16, 36, 4)

    def ghosts(ref):
        for i, vector in enumerate(VELOCITIES):
            for third in range(3):
                if vector[1] > 0:
                    ref[i, third, 0] = roll_lanes(ref[i, third, 8], SEG)
                if vector[1] < 0:
                    ref[i, third, 9] = roll_lanes(ref[i, third, 1], -SEG)

    def streamed(ref, i, third, plane, lane_shift):
        vector = VELOCITIES[i]
        source = third - vector[0]
        value = ref[i, source % 3, plane + 1 - vector[1]]
        if source < 0:
            value = roll_rows(value, 1)
        elif source > 2:
            value = roll_rows(value, -1)
        return roll_lanes(value, vector[2] + lane_shift)

    def start_plane(plane, carry):
        for third in range(3):
            values = [fields[field, third, plane] for field in range(4)]
            result = first_collided(values[0], values[1:], kinds[third, plane])
            for i in range(19):
                old[i, third, plane + 1] = result[i]
        return carry

    lax.fori_loop(0, 8, start_plane, 0)
    ghosts(old)

    source, target = old, new
    for _ in range(STEPS - 1):

        def step_plane(plane, carry, source=source, target=target):
            for third in range(3):
                members = [streamed(source, i, third, plane, 0) for i in range(19)]
                result = collided(members, kinds[third, plane])
                for i in range(19):
                    target[i, third, plane + 1] = result[i]
            return carry

        lax.fori_loop(0, 8, step_plane, 0)
        ghosts(target)
        source, target = target, source

    copies = []
    for i in range(19):
        for third in range(3):
            for plane in range(8):
                for segment in range(3):
                    y = segment * 8 + plane - HALO
                    if 0 <= y < 16:
                        value = streamed(source, i, third, plane, -(segment * SEG + HALO))
                        rows_out[i, pl.ds(third * 16 + y, 8, stride=48), :] = value
        copy = pltpu.make_async_copy(rows_out.at[i, pl.ds(HALO * 16, 256), :], out.at[i], sems.at[i])
        copy.start()
        copies.append(copy)
    for copy in copies:
        copy.wait()


def run_steps(fields, y_low, y_high, kinds):
    return pl.pallas_call(
        steps_kernel,
        out_shape=jax.ShapeDtypeStruct((19, 256, 128), F32),
        in_specs=[pl.BlockSpec(memory_space=pltpu.VMEM)] * 4,
        out_specs=pl.BlockSpec(memory_space=pl.ANY),
        scratch_shapes=[
            pltpu.VMEM((2, 96, 128), F32),
            pltpu.VMEM((4, 3, 8, 8, 128), F32),
            pltpu.VMEM((3, 8, 8, 128), F32),
            pltpu.VMEM((19, 3, 10, 8, 128), F32),
            pltpu.VMEM((19, 3, 10, 8, 128), F32),
            pltpu.VMEM((19, 384, 128), F32),
            pltpu.SemaphoreType.DMA((19,)),
        ],
        compiler_params=pltpu.CompilerParams(vmem_limit_bytes=20 << 20),
        name="run_steps",
    )(fields, y_low, y_high, kinds)


def own_kinds(site_kind):
    kinds = jnp.pad(site_kind.astype(F32), HALO)
    kinds = kinds.reshape(8, 3, 3, 8, SEG).transpose(1, 3, 0, 2, 4).reshape(192, 3 * SEG)
    return jnp.pad(kinds, ((0, 0), (0, 128 - 3 * SEG)))


def on_device(moved_fields, send_slot, recv_index, site_kind):
    kinds = own_kinds(site_kind)
    blocks, low, high = rebalanced(moved_fields, send_slot, recv_index, kinds)
    below = from_before(high, "ba")
    above = from_after(low, "ba")
    kinds, down, up = cross_messages(blocks, below, above, kinds)
    x_low = from_before(up, "gx")
    x_high = from_after(down, "gx")
    kinds, down, up = side_messages(blocks, below, above, x_low, x_high, kinds)
    y_low = from_before(up, "gy")
    y_high = from_after(down, "gy")
    fields = unpacked(blocks, below, above, x_low, x_high)
    out = run_steps(fields, y_low, y_high, kinds)
    return out.reshape(19, 16, 16, 128)[..., :32]


def solution(mesh):
    return jax.shard_map(
        on_device,
        mesh=mesh,
        in_specs=(
            P("gx", "gy", "ba", None, None, None),
            P("gx", "gy", "ba", None, None),
            P("gx", "gy", "ba", None),
            P("gx", "gy", "ba"),
        ),
        out_specs=P(None, "gx", "gy", "ba"),
        check_vma=False,
    )
```

```python
import jax
import jax.numpy as jnp
from jax import lax
from jax.experimental import pallas as pl
from jax.experimental.pallas import tpu as pltpu
from jax.sharding import PartitionSpec as P

STEPS = 4
HALO = 4

VELOCITIES = (
    (0, 0, 0),
    (1, 0, 0),
    (-1, 0, 0),
    (0, 1, 0),
    (0, -1, 0),
    (0, 0, 1),
    (0, 0, -1),
    (1, 1, 0),
    (-1, -1, 0),
    (1, -1, 0),
    (-1, 1, 0),
    (1, 0, 1),
    (-1, 0, -1),
    (1, 0, -1),
    (-1, 0, 1),
    (0, 1, 1),
    (0, -1, -1),
    (0, 1, -1),
    (0, -1, 1),
)
WEIGHTS = (1.0 / 3.0,) + (1.0 / 18.0,) * 6 + (1.0 / 36.0,) * 12
OPPOSITE = (0, 2, 1, 4, 3, 6, 5, 8, 7, 10, 9, 12, 11, 14, 13, 16, 15, 18, 17)
RELAX_RATE = 1.25
INLET_SPEED = 0.05

SEG = 40
F32 = jnp.float32


def shifted_pairs(axis, step):
    devices = lax.axis_size(axis)
    return [(i, (i + step) % devices) for i in range(devices)]


def from_before(array, axis):
    return lax.ppermute(array, axis, shifted_pairs(axis, 1))


def from_after(array, axis):
    return lax.ppermute(array, axis, shifted_pairs(axis, -1))


def lane_ids():
    return lax.broadcasted_iota(jnp.int32, (8, 128), 1)


def row_ids():
    return lax.broadcasted_iota(jnp.int32, (8, 128), 0)


def roll_lanes(value, amount):
    amount = amount % 128
    return value if amount == 0 else pltpu.roll(value, amount, 1)


def kind_rows(third, plane):
    return pl.ds((third * 8 + plane) * 8, 8)


def column_rows(column):
    return pl.ds((column % 3) * 64 + column // 3, 8, stride=8)


def roll_rows(value, amount):
    amount = amount % 8
    return value if amount == 0 else pltpu.roll(value, amount, 0)


RELAY = 5
FIRST_HOPS = {1: (1, 6, -4), 2: (2, 7, -3), -1: (-1, 4, -6), -2: (-2, 3, -7), 3: (8,)}
KEPT = (0, RELAY, -RELAY)
UPWARD = (3, 4, 5, 6, 7, 8)
DOWNWARD = (-8, -7, -6, -5, -4, -3)


def first_hop_pairs(hop):
    if hop != 3:
        return shifted_pairs("gy", hop)
    devices = lax.axis_size("gy")
    return [(i, (i + (3 if i % 2 == 0 else -3)) % devices) for i in range(devices)]


def tiles():
    return [pl.ds(8 * tile, 8) for tile in range(16)]


def gather_kernel(wanted, held, *outs):
    devices = wanted.shape[0]
    me = lax.axis_index("gy")
    for out, offsets in zip(outs, list(FIRST_HOPS.values()) + [KEPT]):
        for place, offset in enumerate(offsets):
            slot = wanted[lax.rem(me + offset + devices, devices)]
            source = jnp.maximum(slot, 0)
            for tile, rows in enumerate(tiles()):
                value = held[source, rows, :]
                if tile == 0:
                    value = jnp.where(slot >= 0, value, 0.0)
                out[place, rows, :] = value


def gather_blocks(wanted, held):
    sizes = [len(offsets) for offsets in FIRST_HOPS.values()] + [len(KEPT)]
    return pl.pallas_call(
        gather_kernel,
        out_shape=[jax.ShapeDtypeStruct((size, 128, 128), F32) for size in sizes],
        in_specs=[
            pl.BlockSpec(memory_space=pltpu.SMEM),
            pl.BlockSpec(memory_space=pltpu.VMEM),
        ],
        out_specs=[pl.BlockSpec(memory_space=pltpu.VMEM)] * len(sizes),
        compiler_params=pltpu.CompilerParams(vmem_limit_bytes=6 << 20),
        name="gather_blocks",
    )(wanted, held)


def merge_kernel(*refs):
    sources, outs = refs[:-2], refs[-2:]
    where = {}
    for source, offsets in zip(sources, list(FIRST_HOPS.values()) + [KEPT]):
        for place, offset in enumerate(offsets):
            where[offset] = (source, place)
    where[-8] = where[8]
    odd = lax.rem(lax.axis_index("gy"), 2)
    for out, offsets, parity in zip(outs, (UPWARD, DOWNWARD), (1, 0)):
        first, second, seen = [], [], None
        for offset in offsets:
            source, place = where[offset]
            live = jnp.broadcast_to(source[place, pl.ds(0, 1), :], (8, 128)) > 0.3
            count = jnp.where(live, 1, 0)
            if abs(offset) == 8:
                count = count * jnp.where(odd == parity, 1, 0)
                live = count > 0
            before = jnp.zeros_like(count) if seen is None else seen
            first.append(live & (before == 0))
            second.append(live & (before == 1))
            seen = before + count
        for rows in tiles():
            values = [where[offset][0][where[offset][1], rows, :] for offset in offsets]
            for place, masks in enumerate((first, second)):
                result = values[0]
                for mask, value in zip(masks[1:], values[1:]):
                    result = jnp.where(mask, value, result)
                out[place, rows, :] = result


def merge_blocks(arrays):
    return pl.pallas_call(
        merge_kernel,
        out_shape=(jax.ShapeDtypeStruct((2, 128, 128), F32),) * 2,
        in_specs=[pl.BlockSpec(memory_space=pltpu.VMEM)] * len(arrays),
        out_specs=(pl.BlockSpec(memory_space=pltpu.VMEM),) * 2,
        compiler_params=pltpu.CompilerParams(vmem_limit_bytes=6 << 20),
        name="merge_blocks",
    )(*arrays)


def pick_kernel(senders, kinds, *refs):
    sources, (from_below, from_above, blocks, low, high) = refs[:-5], refs[-5:]
    devices = lax.axis_size("gy")
    me = lax.axis_index("gy")
    offsets = [lax.rem(me - senders[t] + devices, devices) for t in range(2)]

    def take(condition, source, place, t):
        @pl.when(condition)
        def _():
            for rows in tiles():
                blocks[t, rows, :] = source[place, rows, :]

    for t in range(2):
        offset, other = offsets[t], offsets[1 - t]
        for source, reached in zip(sources, list(FIRST_HOPS) + [0]):
            if reached != 3:
                take(offset == reached % devices, source, 0, t)
        odd = lax.rem(me, 2)
        for source, lowest, highest in (
            (from_below, UPWARD[0], UPWARD[-1] - odd),
            (from_above, DOWNWARD[0] + devices + 1 - odd, DOWNWARD[-1] + devices),
        ):
            place = jnp.where((other >= lowest) & (other < offset), 1, 0)
            take((offset >= lowest) & (offset <= highest), source, place, t)
    part = (lane_ids() % 16) // 4
    for group in range(4):
        first = None
        last = None
        for quarter in range(4):
            rows = pl.ds((group * 4 + quarter) * 8, 8)
            near = roll_lanes(blocks[0, rows, :], 4 * quarter)
            far = roll_lanes(blocks[1, rows, :], 4 * quarter - 12)
            first = near if first is None else jnp.where(part == quarter, near, first)
            last = far if last is None else jnp.where(part == quarter, far, last)
        low[group] = first
        high[group] = last
    part = (lane_ids() % SEG) // 4
    for third in range(3):
        first = None
        last = None
        for plane in range(8):
            value = kinds[kind_rows(third, plane), :]
            near = roll_lanes(value, 4 * plane - 4)
            far = roll_lanes(value, 4 * plane - 32)
            first = near if first is None else jnp.where(part == plane, near, first)
            last = far if last is None else jnp.where(part == plane, far, last)
        low[4 + third] = first
        high[4 + third] = last


def pick_blocks(senders, kinds, arrays):
    return pl.pallas_call(
        pick_kernel,
        out_shape=(
            jax.ShapeDtypeStruct((2, 128, 128), F32),
            jax.ShapeDtypeStruct((7, 8, 128), F32),
            jax.ShapeDtypeStruct((7, 8, 128), F32),
        ),
        in_specs=[
            pl.BlockSpec(memory_space=pltpu.SMEM),
            pl.BlockSpec(memory_space=pltpu.VMEM),
        ]
        + [pl.BlockSpec(memory_space=pltpu.VMEM)] * len(arrays),
        out_specs=(pl.BlockSpec(memory_space=pltpu.VMEM),) * 3,
        compiler_params=pltpu.CompilerParams(vmem_limit_bytes=6 << 20),
        name="pick_blocks",
    )(senders, kinds, *arrays)


def rebalanced(moved_fields, send_slot, recv_index, kinds):
    slots = moved_fields.shape[3]
    held = moved_fields.reshape(slots, 4, 32, 128).transpose(0, 2, 1, 3).reshape(slots, 128, 128)
    wanted = jnp.where(send_slot < 0, -1, send_slot).reshape(-1)
    *messages, kept = gather_blocks(wanted, held)
    arrays = [
        lax.ppermute(message, "gy", first_hop_pairs(hop))
        for hop, message in zip(FIRST_HOPS, messages)
    ] + [kept]
    upward, downward = merge_blocks(arrays)
    from_below = lax.ppermute(upward, "gy", shifted_pairs("gy", RELAY))
    from_above = lax.ppermute(downward, "gy", shifted_pairs("gy", -RELAY))
    return pick_blocks(recv_index.reshape(-1), kinds, arrays + [from_below, from_above])


def cross_kernel(blocks, below, above, kinds, full, down, up):
    place = lane_ids() % SEG
    for third in range(3):
        for plane in range(8):
            value = kinds[kind_rows(third, plane), :]
            value = jnp.where(place < 4, roll_lanes(below[4 + third], -4 * plane), value)
            value = jnp.where(place >= 36, roll_lanes(above[4 + third], 36 - 4 * plane), value)
            full[kind_rows(third, plane), :] = value
    for message, start in ((down, 0), (up, 12)):
        for column in range(4):
            rows = pl.ds((start + column) * 8, 8)
            message[column] = blocks[0, rows, :]
            message[4 + column] = blocks[1, rows, :]
            message[10 + column] = full[column_rows(start + column + HALO), :]
        message[8] = below[start // 4]
        message[9] = above[start // 4]


def cross_messages(blocks, below, above, kinds):
    return pl.pallas_call(
        cross_kernel,
        out_shape=(
            jax.ShapeDtypeStruct((192, 128), F32),
            jax.ShapeDtypeStruct((14, 8, 128), F32),
            jax.ShapeDtypeStruct((14, 8, 128), F32),
        ),
        in_specs=[pl.BlockSpec(memory_space=pltpu.VMEM)] * 4,
        out_specs=(pl.BlockSpec(memory_space=pltpu.VMEM),) * 3,
        compiler_params=pltpu.CompilerParams(vmem_limit_bytes=4 << 20),
        name="cross_messages",
    )(blocks, below, above, kinds)


def row_tiles(blocks, below, above, x_low, x_high):
    entries = []
    for column in range(24):
        if column < 4:
            entries.append((x_low[column], x_low[4 + column]))
        elif column < 20:
            rows = pl.ds((column - 4) * 8, 8)
            entries.append((blocks[0, rows, :], blocks[1, rows, :]))
        else:
            entries.append((x_high[column - 20], x_high[column - 16]))
    for group in range(6):
        if group == 0:
            entries.append((x_low[8], x_low[9]))
        elif group < 5:
            entries.append((below[group - 1], above[group - 1]))
        else:
            entries.append((x_high[8], x_high[9]))
    return entries


def side_kernel(blocks, below, above, x_low, x_high, kinds, full, down, up):
    full[...] = kinds[...]
    for column in range(4):
        full[column_rows(column), :] = x_low[10 + column]
        full[column_rows(20 + column), :] = x_high[10 + column]
    third_of = lane_ids() // SEG
    for y in range(4):
        for message, plane, segment in ((down, y + 4, 0), (up, y, 2)):
            packed = None
            for third in range(3):
                value = roll_lanes(full[kind_rows(third, plane), :], (third - segment) * SEG)
                packed = value if packed is None else jnp.where(third_of == third, value, packed)
            message[pl.ds(120 + 8 * y, 8), :] = packed
    left = lane_ids() < 64
    top = row_ids() < 4
    entries = row_tiles(blocks, below, above, x_low, x_high)
    for pair in range(15):
        first, second = entries[2 * pair], entries[2 * pair + 1]
        a = jnp.where(left, first[0], roll_lanes(first[1], 64))
        b = jnp.where(left, second[0], roll_lanes(second[1], 64))
        down[pl.ds(8 * pair, 8), :] = jnp.where(top, a, roll_rows(b, 4))
        a = jnp.where(left, roll_lanes(first[0], 64), first[1])
        b = jnp.where(left, roll_lanes(second[0], 64), second[1])
        up[pl.ds(8 * pair, 8), :] = jnp.where(top, roll_rows(a, 4), b)


def side_messages(blocks, below, above, x_low, x_high, kinds):
    return pl.pallas_call(
        side_kernel,
        out_shape=(
            jax.ShapeDtypeStruct((192, 128), F32),
            jax.ShapeDtypeStruct((152, 128), F32),
            jax.ShapeDtypeStruct((152, 128), F32),
        ),
        in_specs=[pl.BlockSpec(memory_space=pltpu.VMEM)] * 6,
        out_specs=(pl.BlockSpec(memory_space=pltpu.VMEM),) * 3,
        compiler_params=pltpu.CompilerParams(vmem_limit_bytes=4 << 20),
        name="side_messages",
    )(blocks, below, above, x_low, x_high, kinds)


def dotted(vector, speeds):
    running = None
    for sign_value, component in zip(vector, speeds):
        if sign_value != 0:
            if running is None:
                running = component if sign_value > 0 else -component
            else:
                running = running + component if sign_value > 0 else running - component
    return running


def equilibrium(scale, speeds):
    halves = [0.5 * speed for speed in speeds]
    squared = speeds[0] * speeds[0] + speeds[1] * speeds[1] + speeds[2] * speeds[2]
    baseline = 1.0 - squared * (1.0 / 6.0)
    weighted = {w: scale * w for w in sorted(set(WEIGHTS))}
    based = {w: value * baseline for w, value in weighted.items()}
    pairs = []
    for i in range(1, 19, 2):
        odd = weighted[WEIGHTS[i]] * dotted(VELOCITIES[i], speeds)
        pairs.append((based[WEIGHTS[i]] + odd * dotted(VELOCITIES[i], halves), odd))
    return based[WEIGHTS[0]], pairs


def at_inlet(inlet, speeds):
    return [
        jnp.where(inlet, value, speed)
        for value, speed in zip((0.0, 0.0, 3.0 * INLET_SPEED), speeds)
    ]


def coefficients(kind):
    wall, fixed = kind == 1, kind >= 2
    return (
        jnp.where(wall | fixed, 0.0, RELAX_RATE),
        jnp.where(fixed, 1.0, 0.0),
        jnp.where(wall, 0.5, jnp.where(fixed, 0.0, 0.5 * (1.0 - RELAX_RATE))),
        jnp.where(wall, -0.5, jnp.where(fixed, 0.0, 0.5 * (1.0 - RELAX_RATE))),
    )


def collided(members, kind, factors):
    times, plus, even_kept, odd_kept = factors
    sums = [members[i] + members[i + 1] for i in range(1, 19, 2)]
    differences = [members[i] - members[i + 1] for i in range(1, 19, 2)]
    density = members[0]
    for value in sums:
        density = density + value
    triple = 3.0 / density
    speeds = []
    for axis in range(3):
        momentum = None
        for vector, value in zip(VELOCITIES[1::2], differences):
            if vector[axis] != 0:
                if momentum is None:
                    momentum = value if vector[axis] > 0 else -value
                else:
                    momentum = momentum + value if vector[axis] > 0 else momentum - value
        speeds.append(momentum * triple)
    rest, pairs = equilibrium(density * times + plus, at_inlet(kind == 2, speeds))
    result = [members[0] * (even_kept + even_kept) + rest]
    for (even, odd), total, difference in zip(pairs, sums, differences):
        even = total * even_kept + even
        odd = difference * odd_kept + odd
        result += [even + odd, even - odd]
    return result


def first_collided(density, speeds, kind):
    sign = jnp.where(kind == 1, -3.0, 3.0)
    speeds = at_inlet(kind == 2, [sign * speed for speed in speeds])
    rest, pairs = equilibrium(jnp.where(kind >= 2, 1.0, density), speeds)
    result = [rest]
    for even, odd in pairs:
        result += [even + odd, even - odd]
    return result


def put(fields, field, third, y, value, lane, target, width):
    segment, plane = divmod(y, 8)
    target = segment * SEG + target
    value = roll_lanes(value, target - lane)
    fields[field, third, plane, :, target : target + width] = value[:, target : target + width]


def unpack_kernel(blocks, below, above, x_low, x_high, fields, native):
    for block in range(2):
        native[block, pl.ds(0, 32), :] = x_low[pl.ds(4 * block, 4)].reshape(32, 128)
        native[block, pl.ds(32, 128), :] = blocks[block]
        native[block, pl.ds(160, 32), :] = x_high[pl.ds(4 * block, 4)].reshape(32, 128)
    near = lane_ids() % 16 < 4
    for group in range(6):
        if group == 0:
            lo, hi = x_low[8], x_low[9]
        elif group < 5:
            lo, hi = below[group - 1], above[group - 1]
        else:
            lo, hi = x_high[8], x_high[9]
        for quarter in range(4):
            column = group * 4 + quarter
            native[2, pl.ds(column * 8, 8), :] = jnp.where(
                near, roll_lanes(hi, -4 * quarter), roll_lanes(lo, 12 - 4 * quarter)
            )
    for field in range(4):
        for third in range(3):
            for half in range(2):
                rows = pl.ds(third * 8 + half * 4 + field, 8, stride=24)
                for block in range(2):
                    value = native[block, rows, :]
                    for j in range(8):
                        y = half * 8 + j + 4
                        put(fields, field, third, y, value, j * 16, 4 + 16 * block, 16)
                value = native[2, rows, :]
                for j in range(8):
                    y = half * 8 + j + 4
                    put(fields, field, third, y, value, j * 16 + 12, 0, 4)
                    put(fields, field, third, y, value, j * 16, 36, 4)


def unpacked(blocks, below, above, x_low, x_high):
    return pl.pallas_call(
        unpack_kernel,
        out_shape=jax.ShapeDtypeStruct((4, 3, 8, 8, 128), F32),
        in_specs=[pl.BlockSpec(memory_space=pltpu.VMEM)] * 5,
        out_specs=pl.BlockSpec(memory_space=pltpu.VMEM),
        scratch_shapes=[pltpu.VMEM((3, 192, 128), F32)],
        compiler_params=pltpu.CompilerParams(vmem_limit_bytes=4 << 20),
        cost_estimate=pl.CostEstimate(flops=2000000, bytes_accessed=4000000, transcendentals=0),
        name="unpack",
    )(blocks, below, above, x_low, x_high)


def steps_kernel(
    near_fields, y_low, y_high, near_kinds, out,
    margin, fields, kinds, factors, old, new, rows_out, sems,
):
    lanes = lane_ids()

    for third in range(3):
        for plane in range(8):
            value = near_kinds[kind_rows(third, plane), :]
            if plane < 4:
                side = roll_lanes(y_low[pl.ds(120 + 8 * plane, 8), :], -third * SEG)
                value = jnp.where(lanes < SEG, side, value)
            else:
                side = roll_lanes(y_high[pl.ds(88 + 8 * plane, 8), :], (2 - third) * SEG)
                value = jnp.where(lanes >= 2 * SEG, side, value)
            kinds[third, plane] = value

    for side, message in enumerate((y_low, y_high)):
        for pair in range(3):
            value = message[pl.ds(96 + 8 * pair, 8), :]
            for quarter in range(4):
                rolled = roll_lanes(value, -4 * quarter)
                for half in range(2):
                    column = (2 * pair + half) * 4 + quarter
                    margin[side, pl.ds(column * 4, 4), :] = rolled[4 * half : 4 * half + 4]

    fields[...] = near_fields[...]
    for field in range(4):
        for third in range(3):
            rows = pl.ds(third * 4 + field, 8, stride=12)
            for side, message in enumerate((y_low, y_high)):
                value = message[rows, :]
                for j in range(4):
                    y = 20 * side + j
                    put(fields, field, third, y, value, j * 16, 4, 16)
                    put(fields, field, third, y, value, 64 + j * 16, 20, 16)
                value = margin[side, rows, :]
                for j in range(4):
                    y = 20 * side + j
                    put(fields, field, third, y, value, j * 16, 0, 4)
                    put(fields, field, third, y, value, 64 + j * 16, 36, 4)

    def ghosts(ref):
        for i, vector in enumerate(VELOCITIES):
            for third in range(3):
                if vector[1] > 0:
                    ref[i, third, 0] = roll_lanes(ref[i, third, 8], SEG)
                if vector[1] < 0:
                    ref[i, third, 9] = roll_lanes(ref[i, third, 1], -SEG)

    def streamed(ref, i, third, plane, lane_shift):
        vector = VELOCITIES[i]
        source = third - vector[0]
        value = ref[i, source % 3, plane + 1 - vector[1]]
        if source < 0:
            value = roll_rows(value, 1)
        elif source > 2:
            value = roll_rows(value, -1)
        return roll_lanes(value, vector[2] + lane_shift)

    def start_plane(plane, carry):
        for third in range(3):
            values = [fields[field, third, plane] for field in range(4)]
            result = first_collided(values[0], values[1:], kinds[third, plane])
            for place, value in enumerate(coefficients(kinds[third, plane])):
                factors[place, third, plane] = value
            for i in range(19):
                old[i, third, plane + 1] = result[i]
        return carry

    lax.fori_loop(0, 8, start_plane, 0)
    ghosts(old)

    source, target = old, new
    for _ in range(STEPS - 1):

        def step_plane(plane, carry, source=source, target=target):
            for third in range(3):
                members = [streamed(source, i, third, plane, 0) for i in range(19)]
                known = [factors[place, third, plane] for place in range(4)]
                result = collided(members, kinds[third, plane], known)
                for i in range(19):
                    target[i, third, plane + 1] = result[i]
            return carry

        lax.fori_loop(0, 8, step_plane, 0)
        ghosts(target)
        source, target = target, source

    copies = []
    for i in range(19):
        for third in range(3):
            for plane in range(8):
                for segment in range(3):
                    y = segment * 8 + plane - HALO
                    if 0 <= y < 16:
                        value = streamed(source, i, third, plane, -(segment * SEG + HALO))
                        rows_out[i, pl.ds(third * 16 + y, 8, stride=48), :] = value
        copy = pltpu.make_async_copy(rows_out.at[i, pl.ds(HALO * 16, 256), :], out.at[i], sems.at[i])
        copy.start()
        copies.append(copy)
    for copy in copies:
        copy.wait()


def run_steps(fields, y_low, y_high, kinds):
    return pl.pallas_call(
        steps_kernel,
        out_shape=jax.ShapeDtypeStruct((19, 256, 128), F32),
        in_specs=[pl.BlockSpec(memory_space=pltpu.VMEM)] * 4,
        out_specs=pl.BlockSpec(memory_space=pl.ANY),
        scratch_shapes=[
            pltpu.VMEM((2, 96, 128), F32),
            pltpu.VMEM((4, 3, 8, 8, 128), F32),
            pltpu.VMEM((3, 8, 8, 128), F32),
            pltpu.VMEM((4, 3, 8, 8, 128), F32),
            pltpu.VMEM((19, 3, 10, 8, 128), F32),
            pltpu.VMEM((19, 3, 10, 8, 128), F32),
            pltpu.VMEM((19, 384, 128), F32),
            pltpu.SemaphoreType.DMA((19,)),
        ],
        compiler_params=pltpu.CompilerParams(vmem_limit_bytes=20 << 20),
        name="run_steps",
    )(fields, y_low, y_high, kinds)


def own_kinds(site_kind):
    kinds = jnp.pad(site_kind.astype(F32), HALO)
    kinds = kinds.reshape(8, 3, 3, 8, SEG).transpose(1, 3, 0, 2, 4).reshape(192, 3 * SEG)
    return jnp.pad(kinds, ((0, 0), (0, 128 - 3 * SEG)))


def on_device(moved_fields, send_slot, recv_index, site_kind):
    kinds = own_kinds(site_kind)
    blocks, low, high = rebalanced(moved_fields, send_slot, recv_index, kinds)
    below = from_before(high, "ba")
    above = from_after(low, "ba")
    kinds, down, up = cross_messages(blocks, below, above, kinds)
    x_low = from_before(up, "gx")
    x_high = from_after(down, "gx")
    kinds, down, up = side_messages(blocks, below, above, x_low, x_high, kinds)
    y_low = from_before(up, "gy")
    y_high = from_after(down, "gy")
    fields = unpacked(blocks, below, above, x_low, x_high)
    out = run_steps(fields, y_low, y_high, kinds)
    return out.reshape(19, 16, 16, 128)[..., :32]


def solution(mesh):
    return jax.shard_map(
        on_device,
        mesh=mesh,
        in_specs=(
            P("gx", "gy", "ba", None, None, None),
            P("gx", "gy", "ba", None, None),
            P("gx", "gy", "ba", None),
            P("gx", "gy", "ba"),
        ),
        out_specs=P(None, "gx", "gy", "ba"),
        check_vma=False,
    )
```

```python
import jax
import jax.numpy as jnp
from jax import lax
from jax.experimental import pallas as pl
from jax.experimental.pallas import tpu as pltpu
from jax.sharding import PartitionSpec as P

STEPS = 4
HALO = 4

VELOCITIES = (
    (0, 0, 0),
    (1, 0, 0),
    (-1, 0, 0),
    (0, 1, 0),
    (0, -1, 0),
    (0, 0, 1),
    (0, 0, -1),
    (1, 1, 0),
    (-1, -1, 0),
    (1, -1, 0),
    (-1, 1, 0),
    (1, 0, 1),
    (-1, 0, -1),
    (1, 0, -1),
    (-1, 0, 1),
    (0, 1, 1),
    (0, -1, -1),
    (0, 1, -1),
    (0, -1, 1),
)
WEIGHTS = (1.0 / 3.0,) + (1.0 / 18.0,) * 6 + (1.0 / 36.0,) * 12
OPPOSITE = (0, 2, 1, 4, 3, 6, 5, 8, 7, 10, 9, 12, 11, 14, 13, 16, 15, 18, 17)
RELAX_RATE = 1.25
INLET_SPEED = 0.05

SEG = 40
FRAME = SEG + HALO
F32 = jnp.float32


def shifted_pairs(axis, step):
    devices = lax.axis_size(axis)
    return [(i, (i + step) % devices) for i in range(devices)]


def from_before(array, axis):
    return lax.ppermute(array, axis, shifted_pairs(axis, 1))


def from_after(array, axis):
    return lax.ppermute(array, axis, shifted_pairs(axis, -1))


def lane_ids():
    return lax.broadcasted_iota(jnp.int32, (8, 128), 1)


def row_ids():
    return lax.broadcasted_iota(jnp.int32, (8, 128), 0)


def roll_lanes(value, amount):
    amount = amount % 128
    return value if amount == 0 else pltpu.roll(value, amount, 1)


def kind_rows(third, plane):
    return pl.ds((third * 8 + plane) * 8, 8)


def column_rows(column):
    return pl.ds((column % 3) * 64 + column // 3, 8, stride=8)


def roll_rows(value, amount):
    amount = amount % 8
    return value if amount == 0 else pltpu.roll(value, amount, 0)


RELAY = 5
FIRST_HOPS = {1: (1, 6, -4), 2: (2, 7, -3), -1: (-1, 4, -6), -2: (-2, 3, -7), 3: (8,)}
KEPT = (0, RELAY, -RELAY)
UPWARD = (3, 4, 5, 6, 7, 8)
DOWNWARD = (-8, -7, -6, -5, -4, -3)


def first_hop_pairs(hop):
    if hop != 3:
        return shifted_pairs("gy", hop)
    devices = lax.axis_size("gy")
    return [(i, (i + (3 if i % 2 == 0 else -3)) % devices) for i in range(devices)]


def tiles():
    return [pl.ds(8 * tile, 8) for tile in range(16)]


def gather_kernel(wanted, held, *outs):
    devices = wanted.shape[0]
    me = lax.axis_index("gy")
    for out, offsets in zip(outs, list(FIRST_HOPS.values()) + [KEPT]):
        for place, offset in enumerate(offsets):
            slot = wanted[lax.rem(me + offset + devices, devices)]
            source = jnp.maximum(slot, 0)
            for tile, rows in enumerate(tiles()):
                value = held[source, rows, :]
                if tile == 0:
                    value = jnp.where(slot >= 0, value, 0.0)
                out[place, rows, :] = value


def gather_blocks(wanted, held):
    sizes = [len(offsets) for offsets in FIRST_HOPS.values()] + [len(KEPT)]
    return pl.pallas_call(
        gather_kernel,
        out_shape=[jax.ShapeDtypeStruct((size, 128, 128), F32) for size in sizes],
        in_specs=[
            pl.BlockSpec(memory_space=pltpu.SMEM),
            pl.BlockSpec(memory_space=pltpu.VMEM),
        ],
        out_specs=[pl.BlockSpec(memory_space=pltpu.VMEM)] * len(sizes),
        compiler_params=pltpu.CompilerParams(vmem_limit_bytes=6 << 20),
        name="gather_blocks",
    )(wanted, held)


def merge_kernel(*refs):
    sources, outs = refs[:-2], refs[-2:]
    where = {}
    for source, offsets in zip(sources, list(FIRST_HOPS.values()) + [KEPT]):
        for place, offset in enumerate(offsets):
            where[offset] = (source, place)
    where[-8] = where[8]
    odd = lax.rem(lax.axis_index("gy"), 2)
    for out, offsets, parity in zip(outs, (UPWARD, DOWNWARD), (1, 0)):
        first, second, seen = [], [], None
        for offset in offsets:
            source, place = where[offset]
            live = jnp.broadcast_to(source[place, pl.ds(0, 1), :], (8, 128)) > 0.3
            count = jnp.where(live, 1, 0)
            if abs(offset) == 8:
                count = count * jnp.where(odd == parity, 1, 0)
                live = count > 0
            before = jnp.zeros_like(count) if seen is None else seen
            first.append(live & (before == 0))
            second.append(live & (before == 1))
            seen = before + count
        for rows in tiles():
            values = [where[offset][0][where[offset][1], rows, :] for offset in offsets]
            for place, masks in enumerate((first, second)):
                result = values[0]
                for mask, value in zip(masks[1:], values[1:]):
                    result = jnp.where(mask, value, result)
                out[place, rows, :] = result


def merge_blocks(arrays):
    return pl.pallas_call(
        merge_kernel,
        out_shape=(jax.ShapeDtypeStruct((2, 128, 128), F32),) * 2,
        in_specs=[pl.BlockSpec(memory_space=pltpu.VMEM)] * len(arrays),
        out_specs=(pl.BlockSpec(memory_space=pltpu.VMEM),) * 2,
        compiler_params=pltpu.CompilerParams(vmem_limit_bytes=6 << 20),
        name="merge_blocks",
    )(*arrays)


def pick_kernel(senders, kinds, *refs):
    sources, (from_below, from_above, blocks, low, high) = refs[:-5], refs[-5:]
    devices = lax.axis_size("gy")
    me = lax.axis_index("gy")
    offsets = [lax.rem(me - senders[t] + devices, devices) for t in range(2)]

    def take(condition, source, place, t):
        @pl.when(condition)
        def _():
            for rows in tiles():
                blocks[t, rows, :] = source[place, rows, :]

    for t in range(2):
        offset, other = offsets[t], offsets[1 - t]
        for source, reached in zip(sources, list(FIRST_HOPS) + [0]):
            if reached != 3:
                take(offset == reached % devices, source, 0, t)
        odd = lax.rem(me, 2)
        for source, lowest, highest in (
            (from_below, UPWARD[0], UPWARD[-1] - odd),
            (from_above, DOWNWARD[0] + devices + 1 - odd, DOWNWARD[-1] + devices),
        ):
            place = jnp.where((other >= lowest) & (other < offset), 1, 0)
            take((offset >= lowest) & (offset <= highest), source, place, t)
    part = (lane_ids() % 16) // 4
    for group in range(4):
        first = None
        last = None
        for quarter in range(4):
            rows = pl.ds((group * 4 + quarter) * 8, 8)
            near = roll_lanes(blocks[0, rows, :], 4 * quarter)
            far = roll_lanes(blocks[1, rows, :], 4 * quarter - 12)
            first = near if first is None else jnp.where(part == quarter, near, first)
            last = far if last is None else jnp.where(part == quarter, far, last)
        low[group] = first
        high[group] = last
    part = (lane_ids() % SEG) // 4
    for third in range(3):
        first = None
        last = None
        for plane in range(8):
            value = kinds[kind_rows(third, plane), :]
            near = roll_lanes(value, 4 * plane - 4)
            far = roll_lanes(value, 4 * plane - 32)
            first = near if first is None else jnp.where(part == plane, near, first)
            last = far if last is None else jnp.where(part == plane, far, last)
        low[4 + third] = first
        high[4 + third] = last


def pick_blocks(senders, kinds, arrays):
    return pl.pallas_call(
        pick_kernel,
        out_shape=(
            jax.ShapeDtypeStruct((2, 128, 128), F32),
            jax.ShapeDtypeStruct((7, 8, 128), F32),
            jax.ShapeDtypeStruct((7, 8, 128), F32),
        ),
        in_specs=[
            pl.BlockSpec(memory_space=pltpu.SMEM),
            pl.BlockSpec(memory_space=pltpu.VMEM),
        ]
        + [pl.BlockSpec(memory_space=pltpu.VMEM)] * len(arrays),
        out_specs=(pl.BlockSpec(memory_space=pltpu.VMEM),) * 3,
        compiler_params=pltpu.CompilerParams(vmem_limit_bytes=6 << 20),
        name="pick_blocks",
    )(senders, kinds, *arrays)


def rebalanced(moved_fields, send_slot, recv_index, kinds):
    slots = moved_fields.shape[3]
    held = moved_fields.reshape(slots, 4, 32, 128).transpose(0, 2, 1, 3).reshape(slots, 128, 128)
    wanted = jnp.where(send_slot < 0, -1, send_slot).reshape(-1)
    *messages, kept = gather_blocks(wanted, held)
    arrays = [
        lax.ppermute(message, "gy", first_hop_pairs(hop))
        for hop, message in zip(FIRST_HOPS, messages)
    ] + [kept]
    upward, downward = merge_blocks(arrays)
    from_below = lax.ppermute(upward, "gy", shifted_pairs("gy", RELAY))
    from_above = lax.ppermute(downward, "gy", shifted_pairs("gy", -RELAY))
    return pick_blocks(recv_index.reshape(-1), kinds, arrays + [from_below, from_above])


def cross_kernel(blocks, below, above, kinds, full, down, up):
    place = lane_ids() % SEG
    for third in range(3):
        for plane in range(8):
            value = kinds[kind_rows(third, plane), :]
            value = jnp.where(place < 4, roll_lanes(below[4 + third], -4 * plane), value)
            value = jnp.where(place >= 36, roll_lanes(above[4 + third], 36 - 4 * plane), value)
            full[kind_rows(third, plane), :] = value
    for message, start in ((down, 0), (up, 12)):
        for column in range(4):
            rows = pl.ds((start + column) * 8, 8)
            message[column] = blocks[0, rows, :]
            message[4 + column] = blocks[1, rows, :]
            message[10 + column] = full[column_rows(start + column + HALO), :]
        message[8] = below[start // 4]
        message[9] = above[start // 4]


def cross_messages(blocks, below, above, kinds):
    return pl.pallas_call(
        cross_kernel,
        out_shape=(
            jax.ShapeDtypeStruct((192, 128), F32),
            jax.ShapeDtypeStruct((14, 8, 128), F32),
            jax.ShapeDtypeStruct((14, 8, 128), F32),
        ),
        in_specs=[pl.BlockSpec(memory_space=pltpu.VMEM)] * 4,
        out_specs=(pl.BlockSpec(memory_space=pltpu.VMEM),) * 3,
        compiler_params=pltpu.CompilerParams(vmem_limit_bytes=4 << 20),
        name="cross_messages",
    )(blocks, below, above, kinds)


def row_tiles(blocks, below, above, x_low, x_high):
    entries = []
    for column in range(24):
        if column < 4:
            entries.append((x_low[column], x_low[4 + column]))
        elif column < 20:
            rows = pl.ds((column - 4) * 8, 8)
            entries.append((blocks[0, rows, :], blocks[1, rows, :]))
        else:
            entries.append((x_high[column - 20], x_high[column - 16]))
    for group in range(6):
        if group == 0:
            entries.append((x_low[8], x_low[9]))
        elif group < 5:
            entries.append((below[group - 1], above[group - 1]))
        else:
            entries.append((x_high[8], x_high[9]))
    return entries


def side_kernel(blocks, below, above, x_low, x_high, kinds, full, down, up):
    full[...] = kinds[...]
    for column in range(4):
        full[column_rows(column), :] = x_low[10 + column]
        full[column_rows(20 + column), :] = x_high[10 + column]
    third_of = lane_ids() // SEG
    for y in range(4):
        for message, plane, segment in ((down, y + 4, 0), (up, y, 2)):
            packed = None
            for third in range(3):
                value = roll_lanes(full[kind_rows(third, plane), :], (third - segment) * SEG)
                packed = value if packed is None else jnp.where(third_of == third, value, packed)
            message[pl.ds(120 + 8 * y, 8), :] = packed
    left = lane_ids() < 64
    top = row_ids() < 4
    entries = row_tiles(blocks, below, above, x_low, x_high)
    for pair in range(15):
        first, second = entries[2 * pair], entries[2 * pair + 1]
        a = jnp.where(left, first[0], roll_lanes(first[1], 64))
        b = jnp.where(left, second[0], roll_lanes(second[1], 64))
        down[pl.ds(8 * pair, 8), :] = jnp.where(top, a, roll_rows(b, 4))
        a = jnp.where(left, roll_lanes(first[0], 64), first[1])
        b = jnp.where(left, roll_lanes(second[0], 64), second[1])
        up[pl.ds(8 * pair, 8), :] = jnp.where(top, roll_rows(a, 4), b)


def side_messages(blocks, below, above, x_low, x_high, kinds):
    return pl.pallas_call(
        side_kernel,
        out_shape=(
            jax.ShapeDtypeStruct((192, 128), F32),
            jax.ShapeDtypeStruct((152, 128), F32),
            jax.ShapeDtypeStruct((152, 128), F32),
        ),
        in_specs=[pl.BlockSpec(memory_space=pltpu.VMEM)] * 6,
        out_specs=(pl.BlockSpec(memory_space=pltpu.VMEM),) * 3,
        compiler_params=pltpu.CompilerParams(vmem_limit_bytes=4 << 20),
        name="side_messages",
    )(blocks, below, above, x_low, x_high, kinds)


def dotted(vector, speeds):
    running = None
    for sign_value, component in zip(vector, speeds):
        if sign_value != 0:
            if running is None:
                running = component if sign_value > 0 else -component
            else:
                running = running + component if sign_value > 0 else running - component
    return running


def equilibrium(scale, speeds):
    halves = [0.5 * speed for speed in speeds]
    squared = speeds[0] * speeds[0] + speeds[1] * speeds[1] + speeds[2] * speeds[2]
    baseline = 1.0 - squared * (1.0 / 6.0)
    weighted = {w: scale * w for w in sorted(set(WEIGHTS))}
    based = {w: value * baseline for w, value in weighted.items()}
    pairs = []
    for i in range(1, 19, 2):
        odd = weighted[WEIGHTS[i]] * dotted(VELOCITIES[i], speeds)
        pairs.append((based[WEIGHTS[i]] + odd * dotted(VELOCITIES[i], halves), odd))
    return based[WEIGHTS[0]], pairs


def at_inlet(inlet, speeds):
    return [
        jnp.where(inlet, value, speed)
        for value, speed in zip((0.0, 0.0, 3.0 * INLET_SPEED), speeds)
    ]


def coefficients(kind):
    wall, fixed = kind == 1, kind >= 2
    return (
        jnp.where(wall | fixed, 0.0, RELAX_RATE),
        jnp.where(fixed, 1.0, 0.0),
        jnp.where(wall, 0.5, jnp.where(fixed, 0.0, 0.5 * (1.0 - RELAX_RATE))),
        jnp.where(wall, -0.5, jnp.where(fixed, 0.0, 0.5 * (1.0 - RELAX_RATE))),
    )


def collided(members, kind, factors):
    times, plus, even_kept, odd_kept = factors
    sums = [members[i] + members[i + 1] for i in range(1, 19, 2)]
    differences = [members[i] - members[i + 1] for i in range(1, 19, 2)]
    density = members[0]
    for value in sums:
        density = density + value
    triple = 3.0 / density
    speeds = []
    for axis in range(3):
        momentum = None
        for vector, value in zip(VELOCITIES[1::2], differences):
            if vector[axis] != 0:
                if momentum is None:
                    momentum = value if vector[axis] > 0 else -value
                else:
                    momentum = momentum + value if vector[axis] > 0 else momentum - value
        speeds.append(momentum * triple)
    rest, pairs = equilibrium(density * times + plus, at_inlet(kind == 2, speeds))
    result = [members[0] * (even_kept + even_kept) + rest]
    for (even, odd), total, difference in zip(pairs, sums, differences):
        even = total * even_kept + even
        odd = difference * odd_kept + odd
        result += [even + odd, even - odd]
    return result


def first_collided(density, speeds, kind):
    sign = jnp.where(kind == 1, -3.0, 3.0)
    speeds = at_inlet(kind == 2, [sign * speed for speed in speeds])
    rest, pairs = equilibrium(jnp.where(kind >= 2, 1.0, density), speeds)
    result = [rest]
    for even, odd in pairs:
        result += [even + odd, even - odd]
    return result


def put(fields, field, third, y, value, lane, target, width):
    segment, plane = divmod(y, 8)
    target = (segment * SEG + target - FRAME) % 128
    value = roll_lanes(value, target - lane)
    fields[field, third, plane, :, target : target + width] = value[:, target : target + width]


def unpack_kernel(blocks, below, above, x_low, x_high, fields, native):
    for block in range(2):
        native[block, pl.ds(0, 32), :] = x_low[pl.ds(4 * block, 4)].reshape(32, 128)
        native[block, pl.ds(32, 128), :] = blocks[block]
        native[block, pl.ds(160, 32), :] = x_high[pl.ds(4 * block, 4)].reshape(32, 128)
    near = lane_ids() % 16 < 4
    for group in range(6):
        if group == 0:
            lo, hi = x_low[8], x_low[9]
        elif group < 5:
            lo, hi = below[group - 1], above[group - 1]
        else:
            lo, hi = x_high[8], x_high[9]
        for quarter in range(4):
            column = group * 4 + quarter
            native[2, pl.ds(column * 8, 8), :] = jnp.where(
                near, roll_lanes(hi, -4 * quarter), roll_lanes(lo, 12 - 4 * quarter)
            )
    for field in range(4):
        for third in range(3):
            for half in range(2):
                rows = pl.ds(third * 8 + half * 4 + field, 8, stride=24)
                for block in range(2):
                    value = native[block, rows, :]
                    for j in range(8):
                        y = half * 8 + j + 4
                        put(fields, field, third, y, value, j * 16, 4 + 16 * block, 16)
                value = native[2, rows, :]
                for j in range(8):
                    y = half * 8 + j + 4
                    put(fields, field, third, y, value, j * 16 + 12, 0, 4)
                    put(fields, field, third, y, value, j * 16, 36, 4)


def unpacked(blocks, below, above, x_low, x_high):
    return pl.pallas_call(
        unpack_kernel,
        out_shape=jax.ShapeDtypeStruct((4, 3, 8, 8, 128), F32),
        in_specs=[pl.BlockSpec(memory_space=pltpu.VMEM)] * 5,
        out_specs=pl.BlockSpec(memory_space=pltpu.VMEM),
        scratch_shapes=[pltpu.VMEM((3, 192, 128), F32)],
        compiler_params=pltpu.CompilerParams(vmem_limit_bytes=4 << 20),
        cost_estimate=pl.CostEstimate(flops=2000000, bytes_accessed=4000000, transcendentals=0),
        name="unpack",
    )(blocks, below, above, x_low, x_high)


def steps_kernel(
    near_fields, y_low, y_high, near_kinds, out,
    margin, fields, kinds, factors, old, new, rows_out, sems,
):
    lanes = lane_ids()

    for third in range(3):
        for plane in range(8):
            value = near_kinds[kind_rows(third, plane), :]
            if plane < 4:
                side = roll_lanes(y_low[pl.ds(120 + 8 * plane, 8), :], -third * SEG)
                value = jnp.where(lanes < SEG, side, value)
            else:
                side = roll_lanes(y_high[pl.ds(88 + 8 * plane, 8), :], (2 - third) * SEG)
                value = jnp.where(lanes >= 2 * SEG, side, value)
            kinds[third, plane] = roll_lanes(value, -FRAME)

    for side, message in enumerate((y_low, y_high)):
        for pair in range(3):
            value = message[pl.ds(96 + 8 * pair, 8), :]
            for quarter in range(4):
                rolled = roll_lanes(value, -4 * quarter)
                for half in range(2):
                    column = (2 * pair + half) * 4 + quarter
                    margin[side, pl.ds(column * 4, 4), :] = rolled[4 * half : 4 * half + 4]

    fields[...] = near_fields[...]
    for field in range(4):
        for third in range(3):
            rows = pl.ds(third * 4 + field, 8, stride=12)
            for side, message in enumerate((y_low, y_high)):
                value = message[rows, :]
                for j in range(4):
                    y = 20 * side + j
                    put(fields, field, third, y, value, j * 16, 4, 16)
                    put(fields, field, third, y, value, 64 + j * 16, 20, 16)
                value = margin[side, rows, :]
                for j in range(4):
                    y = 20 * side + j
                    put(fields, field, third, y, value, j * 16, 0, 4)
                    put(fields, field, third, y, value, 64 + j * 16, 36, 4)

    def ghosts(ref):
        for i, vector in enumerate(VELOCITIES):
            for third in range(3):
                if vector[1] > 0:
                    ref[i, third, 0] = roll_lanes(ref[i, third, 8], SEG)
                if vector[1] < 0:
                    ref[i, third, 9] = roll_lanes(ref[i, third, 1], -SEG)

    def streamed(ref, i, third, plane, lane_shift):
        vector = VELOCITIES[i]
        source = third - vector[0]
        value = ref[i, source % 3, plane + 1 - vector[1]]
        if source < 0:
            value = roll_rows(value, 1)
        elif source > 2:
            value = roll_rows(value, -1)
        return roll_lanes(value, vector[2] + lane_shift)

    def start_plane(plane, carry):
        for third in range(3):
            values = [fields[field, third, plane] for field in range(4)]
            result = first_collided(values[0], values[1:], kinds[third, plane])
            for place, value in enumerate(coefficients(kinds[third, plane])):
                factors[place, third, plane] = value
            for i in range(19):
                old[i, third, plane + 1] = result[i]
        return carry

    lax.fori_loop(0, 8, start_plane, 0)
    ghosts(old)

    source, target = old, new
    for _ in range(STEPS - 1):

        def step_plane(plane, carry, source=source, target=target):
            for third in range(3):
                members = [streamed(source, i, third, plane, 0) for i in range(19)]
                known = [factors[place, third, plane] for place in range(4)]
                result = collided(members, kinds[third, plane], known)
                for i in range(19):
                    target[i, third, plane + 1] = result[i]
            return carry

        lax.fori_loop(0, 8, step_plane, 0)
        ghosts(target)
        source, target = target, source

    copies = []
    for i in range(19):
        for third in range(3):
            for plane in range(8):
                for segment in range(3):
                    y = segment * 8 + plane - HALO
                    if 0 <= y < 16:
                        value = streamed(source, i, third, plane, FRAME - segment * SEG - HALO)
                        rows = rows_out.at[i, y // 8].reshape(192, 128)
                        rows[pl.ds(third * 8 + y % 8, 8, stride=24), :] = value
        for half in range(2):
            copy = pltpu.make_async_copy(
                rows_out.at[i, half, pl.ds(HALO, 16)],
                out.at[i, :, pl.ds(8 * half, 8), :],
                sems.at[i, half],
            )
            copy.start()
            copies.append(copy)
    for copy in copies:
        copy.wait()


def run_steps(fields, y_low, y_high, kinds):
    return pl.pallas_call(
        steps_kernel,
        out_shape=jax.ShapeDtypeStruct((19, 16, 16, 128), F32),
        in_specs=[pl.BlockSpec(memory_space=pltpu.VMEM)] * 4,
        out_specs=pl.BlockSpec(memory_space=pl.ANY),
        scratch_shapes=[
            pltpu.VMEM((2, 96, 128), F32),
            pltpu.VMEM((4, 3, 8, 8, 128), F32),
            pltpu.VMEM((3, 8, 8, 128), F32),
            pltpu.VMEM((4, 3, 8, 8, 128), F32),
            pltpu.VMEM((19, 3, 10, 8, 128), F32),
            pltpu.VMEM((19, 3, 10, 8, 128), F32),
            pltpu.VMEM((19, 2, 24, 8, 128), F32),
            pltpu.SemaphoreType.DMA((19, 2)),
        ],
        compiler_params=pltpu.CompilerParams(vmem_limit_bytes=20 << 20),
        name="run_steps",
    )(fields, y_low, y_high, kinds)


def own_kinds(site_kind):
    kinds = jnp.pad(site_kind.astype(F32), HALO)
    kinds = kinds.reshape(8, 3, 3, 8, SEG).transpose(1, 3, 0, 2, 4).reshape(192, 3 * SEG)
    return jnp.pad(kinds, ((0, 0), (0, 128 - 3 * SEG)))


def on_device(moved_fields, send_slot, recv_index, site_kind):
    kinds = own_kinds(site_kind)
    blocks, low, high = rebalanced(moved_fields, send_slot, recv_index, kinds)
    below = from_before(high, "ba")
    above = from_after(low, "ba")
    kinds, down, up = cross_messages(blocks, below, above, kinds)
    x_low = from_before(up, "gx")
    x_high = from_after(down, "gx")
    kinds, down, up = side_messages(blocks, below, above, x_low, x_high, kinds)
    y_low = from_before(up, "gy")
    y_high = from_after(down, "gy")
    fields = unpacked(blocks, below, above, x_low, x_high)
    out = run_steps(fields, y_low, y_high, kinds)
    return out[..., :32]


def solution(mesh):
    return jax.shard_map(
        on_device,
        mesh=mesh,
        in_specs=(
            P("gx", "gy", "ba", None, None, None),
            P("gx", "gy", "ba", None, None),
            P("gx", "gy", "ba", None),
            P("gx", "gy", "ba"),
        ),
        out_specs=P(None, "gx", "gy", "ba"),
        check_vma=False,
    )
```
